128 devices in a mesh: gx: 8 (over z, core), gy: 16 (over y, x).
Axes of the slice: x: 4, y: 4, z: 4, core: 2. Of those that a mesh axis runs over, the one named last changes fastest.
Arguments:
- velocity: float32 [3, 64, 256, 256], P(None, 'gx', 'gy'), may hold values from -3 to 3
- stress: float32 [6, 64, 256, 256], P(None, 'gx', 'gy'), may hold values from -3 to 3
- materials: float32 [3, 64, 256, 256], P(None, 'gx', 'gy'), may hold values from 0.5 to 1.5
- background_traction: float32 [2, 8, 256, 256], P(None, 'gx', 'gy'), may hold values from -4 to 4
- normal_load: float32 [8, 256, 256], P('gx', 'gy'), may hold values from 1 to 3
- initial_slip: float32 [8, 256, 256], P('gx', 'gy'), may hold values from 0 to 4.5
- static_friction: float32 [8, 32], P('gx'), may hold values from 0.5 to 0.8
- dynamic_friction: float32 [8, 32], P('gx'), may hold values from 0.1 to 0.4
- weakening_slip: float32 [8, 32], P('gx'), may hold values from 0.5 to 2
- segment_blocks: int32 [8, 32, 63], P('gx'), may hold values from 0 to 512, as said below
Outputs:
- velocity_out: float32 [3, 64, 256, 256], P(None, 'gx', 'gy')
- stress_out: float32 [6, 64, 256, 256], P(None, 'gx', 'gy')
- slip_out: float32 [8, 256, 256], P('gx', 'gy')
The draws below stay inside these ranges and needn't reach their ends.
Inputs may be any that keep to these rules, and one draw needn't show every extreme that they name: `segment_blocks`: for each fault the lists hold every block id from 0 to 511 exactly once, each list's ids first and 512 as padding after them; every list holds at least one id and some list exactly 63. Lists 2 o and 2 o + 1 are those of friction owner o, the device of index o along gy. Block b lies on the face of the device of index b // 32 along gy. Of each fault, one group holds exactly 4 blocks of every device's face; every other group holds between 1 and 4 blocks of each face, and the counts of one face over those groups differ by at most one.
All inputs are finite; a program needn't handle non-finite values.
Results may differ from the reference program's by a relative error of at most 0.0001.
Values sent between devices are 32-bit elements; how exact they have to be, the bound alone decides.
A program may use at most 64 MiB of HBM per device.

```python
import math
import jax
import jax.numpy as jnp
from jax import lax

CX = 8
NZ = 256
STEPS = 16
BLOCK = 128
FAULTS = 8
NX = 64
NY = 256
BLOCKS_DEV = 32
FAULT_BLOCKS = 512
CAP = 4
SEGS = 32
MAXB = 63
N_GY = 16


def face_order(order_key):
    return jax.random.permutation(order_key, BLOCKS_DEV)


def fault_lists(fault_key):
    keys = jax.random.split(fault_key, 5)
    full_owner = jax.random.randint(keys[0], (), 0, N_GY)
    orders = jax.vmap(face_order)(jax.random.split(keys[1], N_GY))
    offsets = jax.random.randint(keys[2], (N_GY,), 0, N_GY - 1)
    position = jnp.arange(BLOCKS_DEV, dtype=jnp.int32)
    other_index = (position[None, :] - CAP + offsets[:, None]) % (N_GY - 1)
    other_owner = other_index + (other_index >= full_owner).astype(jnp.int32)
    slot_owner = jnp.where(position[None, :] < CAP, full_owner, other_owner).astype(jnp.int32)
    source_rows = jnp.broadcast_to(jnp.arange(N_GY, dtype=jnp.int32)[:, None], (N_GY, BLOCKS_DEV))
    owner_local = jnp.zeros((N_GY, BLOCKS_DEV), jnp.int32).at[source_rows, orders].set(slot_owner)
    owner_flat = owner_local.reshape(-1)
    shuffled = jax.random.permutation(keys[3], FAULT_BLOCKS).astype(jnp.int32)
    sort_key = owner_flat[shuffled] * FAULT_BLOCKS + jnp.arange(FAULT_BLOCKS, dtype=jnp.int32)
    grouped = shuffled[jnp.argsort(sort_key)]
    loads = jnp.sum((owner_flat[None, :] == jnp.arange(N_GY, dtype=jnp.int32)[:, None]).astype(jnp.int32), axis=1)
    starts = jnp.cumsum(loads) - loads
    cuts = 1 + jax.random.randint(keys[4], (N_GY,), 0, loads - 1)
    cuts = jnp.where(jnp.arange(N_GY) == full_owner, 1, cuts).astype(jnp.int32)
    seg_start = jnp.stack([starts, starts + cuts], axis=1).reshape(-1)
    seg_length = jnp.stack([cuts, loads - cuts], axis=1).reshape(-1)
    column = jnp.arange(MAXB, dtype=jnp.int32)
    picked = grouped[jnp.clip(seg_start[:, None] + column[None, :], 0, FAULT_BLOCKS - 1)]
    return jnp.where(column[None, :] < seg_length[:, None], picked, FAULT_BLOCKS).astype(jnp.int32)


def draw_segment_blocks(key, part):
    base = jax.random.fold_in(key, 7)
    return jax.vmap(fault_lists)(jax.random.split(base, FAULTS))


def draw_initial_slip(key, part):
    strike = jnp.arange(NY, dtype=jnp.float32)[None, :, None] / NY
    values = jax.random.uniform(key, (FAULTS, NY, NZ), jnp.float32, 0.2, 1.5)
    rising = 1.0 + 2.0 * strike
    return (values * rising).astype(jnp.float32)


def block_levels(rng, shape, cuts, smallest, largest):
    level, own = 1.0, jax.random.fold_in(rng, 6)
    for axis_at, blocks in cuts:
        steps = jnp.exp(jax.random.uniform(jax.random.fold_in(own, axis_at), (blocks,), jnp.float32, smallest / len(cuts), largest / len(cuts)))
        level = level * jnp.repeat(steps, shape[axis_at] // blocks).reshape([-1 if axis == axis_at else 1 for axis in range(len(shape))])
    return level


def noise(own_key, dims, width, most, shards=(), held_as=jnp.bfloat16):
    entries = width * jax.random.normal(own_key, dims, jnp.float32)
    if shards:
        entries = entries * block_levels(own_key, dims, shards, -0.22, 0.18)
    return jnp.clip(entries, -most, most).astype(held_as)


def setup_inputs(seed: int = 0) -> dict:
    key_of = jax.random.split(jax.random.key(seed), 11)
    return {
        "velocity": noise(key_of[0], (3, NX, NY, NZ), 0.5, 3.0, ((1, 8), (2, 16)), jnp.float32),
        "stress": noise(key_of[1], (6, NX, NY, NZ), 0.5, 3.0, ((1, 8), (2, 16)), jnp.float32),
        "materials": jnp.clip(jnp.exp(math.log(1.5) - 1.0986123 * jax.random.uniform(key_of[2], (3, NX, NY, NZ), jnp.float32) ** block_levels(key_of[2], (3, NX, NY, NZ), ((1, 8), (2, 16)), -0.2, 0.2)), 0.5, 1.5),
        "background_traction": noise(key_of[3], (2, FAULTS, NY, NZ), 1.0, 4.0, ((1, 8), (2, 16)), jnp.float32),
        "normal_load": jnp.clip(jnp.exp(math.log(3.0) - 1.0986123 * jax.random.uniform(key_of[4], (FAULTS, NY, NZ), jnp.float32) ** block_levels(key_of[4], (FAULTS, NY, NZ), ((0, 8), (1, 16)), -0.2, 0.2)), 1.0, 3.0),
        "initial_slip": draw_initial_slip(jax.random.fold_in(key_of[10], 71), 0),
        "static_friction": jnp.clip(0.5 + 0.3 * jax.random.uniform(key_of[6], (FAULTS, SEGS), jnp.float32) ** block_levels(key_of[6], (FAULTS, SEGS), ((0, 8),), -0.2, 0.2), 0.5, 0.8),
        "dynamic_friction": jnp.clip(0.1 + 0.3 * jax.random.uniform(key_of[7], (FAULTS, SEGS), jnp.float32) ** block_levels(key_of[7], (FAULTS, SEGS), ((0, 8),), -0.2, 0.2), 0.1, 0.4),
        "weakening_slip": jnp.clip(jnp.exp(math.log(2.0) - 1.3862944 * jax.random.uniform(key_of[8], (FAULTS, SEGS), jnp.float32) ** block_levels(key_of[8], (FAULTS, SEGS), ((0, 8),), -0.2, 0.2)), 0.5, 2.0),
        "segment_blocks": draw_segment_blocks(jax.random.fold_in(key_of[10], 71), 0),
    }


time_step = 0.1

def forward_diff(field, axis):
    if axis == 2:
        upper = jnp.concatenate([field[:, :, 1:], jnp.zeros_like(field[:, :, :1])], axis=2)
    else:
        upper = jnp.roll(field, -1, axis)
    return upper - field

def backward_diff(field, axis):
    if axis == 2:
        lower = jnp.concatenate([jnp.zeros_like(field[:, :, :1]), field[:, :, :-1]], axis=2)
    else:
        lower = jnp.roll(field, 1, axis)
    return field - lower

def reference(velocity, stress, materials, background_traction, normal_load, initial_slip, static_friction, dynamic_friction, weakening_slip, segment_blocks):
    lame = materials[0]
    shear = materials[1]
    buoyancy = materials[2]
    modulus = lame + 2.0 * shear
    flat_lists = segment_blocks.reshape(FAULTS, SEGS * MAXB)
    entry_segment = jnp.broadcast_to(jnp.arange(SEGS, dtype=jnp.int32)[:, None], (SEGS, MAXB)).reshape(-1)
    fault_rows = jnp.arange(FAULTS, dtype=jnp.int32)[:, None]
    block_segment = jnp.zeros((FAULTS, FAULT_BLOCKS + 1), jnp.int32).at[fault_rows, flat_lists].set(jnp.broadcast_to(entry_segment[None, :], flat_lists.shape))[:, :FAULT_BLOCKS]
    list_counts = lax.optimization_barrier(jnp.sum(segment_blocks < FAULT_BLOCKS, axis=2)).astype(jnp.float32)
    face_shear = shear[::CX]
    load_blocks = normal_load.reshape(FAULTS, FAULT_BLOCKS, BLOCK)
    vel_x, vel_y, vel_z = (velocity[0], velocity[1], velocity[2])
    str_xx, str_yy, str_zz = (stress[0], stress[1], stress[2])
    str_xy, str_xz, str_yz = (stress[3], stress[4], stress[5])
    slip = initial_slip
    for step_index in range(STEPS):
        accel_x = backward_diff(str_xx, 0) + forward_diff(str_xy, 1) + forward_diff(str_xz, 2)
        accel_y = forward_diff(str_xy, 0) + backward_diff(str_yy, 1) + forward_diff(str_yz, 2)
        accel_z = forward_diff(str_xz, 0) + forward_diff(str_yz, 1) + backward_diff(str_zz, 2)
        vel_x = vel_x + time_step * buoyancy * accel_x
        vel_y = vel_y + time_step * buoyancy * accel_y
        vel_z = vel_z + time_step * buoyancy * accel_z
        strain_x = forward_diff(vel_x, 0)
        strain_y = forward_diff(vel_y, 1)
        strain_z = forward_diff(vel_z, 2)
        str_xx = str_xx + time_step * (modulus * strain_x + lame * (strain_y + strain_z))
        str_yy = str_yy + time_step * (modulus * strain_y + lame * (strain_x + strain_z))
        str_zz = str_zz + time_step * (modulus * strain_z + lame * (strain_x + strain_y))
        str_xy = str_xy + time_step * shear * (backward_diff(vel_y, 0) + backward_diff(vel_x, 1))
        str_xz = str_xz + time_step * shear * (backward_diff(vel_z, 0) + backward_diff(vel_x, 2))
        str_yz = str_yz + time_step * shear * (backward_diff(vel_z, 1) + backward_diff(vel_y, 2))
        trial_y = str_xy[::CX] + background_traction[0]
        trial_z = str_xz[::CX] + background_traction[1]
        magnitude = jnp.sqrt(trial_y * trial_y + trial_z * trial_z)
        block_sums = lax.optimization_barrier(jnp.sum(slip.reshape(FAULTS, FAULT_BLOCKS, BLOCK), axis=2))
        padded_sums = jnp.concatenate([block_sums, jnp.zeros((FAULTS, 1), jnp.float32)], axis=1)
        segment_sums = lax.optimization_barrier(jnp.sum(jnp.take_along_axis(padded_sums, flat_lists, axis=1).reshape(FAULTS, SEGS, MAXB), axis=2))
        mean_slip = segment_sums / (BLOCK * list_counts)
        friction = dynamic_friction + (static_friction - dynamic_friction) * jnp.exp(-mean_slip / weakening_slip)
        block_friction = jnp.take_along_axis(friction, block_segment, axis=1)
        strength = (block_friction[:, :, None] * load_blocks).reshape(FAULTS, NY, NZ)
        excess = 1.0 - strength / jnp.maximum(magnitude, strength)
        str_xy = str_xy.at[::CX].add(-trial_y * excess)
        str_xz = str_xz.at[::CX].add(-trial_z * excess)
        slip = slip + magnitude * excess / face_shear
    velocity_out = jnp.stack([vel_x, vel_y, vel_z])
    stress_out = jnp.stack([str_xx, str_yy, str_zz, str_xy, str_xz, str_yz])
    return (velocity_out, stress_out, slip)
```

```python
import jax
import jax.numpy as jnp
from jax import lax
from jax.experimental import pallas as pl
from jax.experimental.pallas import tpu as pltpu
from jax.sharding import PartitionSpec as P

STEPS = 16
DT = 0.1
GX, GY, NX4 = 8, 16, 4
CX, NY, NZ = 8, 16, 256
LANES = 128
BLOCKS = NY * NZ // LANES
TOTAL = BLOCKS * GY
SEGS, MAXB = 32, 63
MESH = pl.DeviceIdType.MESH

XLO, XHI, YLO, YHI, C0, C1, C2, C3, SUMS = range(9)


def nodes(face):
    return jnp.concatenate([face[:, :LANES], face[:, LANES:]], axis=0)


def face_of(rows):
    return jnp.concatenate([rows[:NY], rows[NY:]], axis=1)


def lane_ids(rows):
    return lax.broadcasted_iota(jnp.int32, (rows, LANES), 1)


def up_z(f):
    lane = lane_ids(f.shape[0])
    a, b = f[:, :LANES], f[:, LANES:]
    ra, rb = pltpu.roll(a, LANES - 1, 1), pltpu.roll(b, LANES - 1, 1)
    last = lane == LANES - 1
    return jnp.concatenate([jnp.where(last, rb, ra), jnp.where(last, 0.0, rb)], axis=1)


def dn_z(f):
    lane = lane_ids(f.shape[0])
    a, b = f[:, :LANES], f[:, LANES:]
    ra, rb = pltpu.roll(a, 1, 1), pltpu.roll(b, 1, 1)
    first = lane == 0
    return jnp.concatenate([jnp.where(first, 0.0, ra), jnp.where(first, ra, rb)], axis=1)


def row_ids():
    return lax.broadcasted_iota(jnp.int32, (8, NZ), 0)


def up_y(f, halo):
    last = row_ids() == 7
    r0, r1 = pltpu.roll(f[:8], 7, 0), pltpu.roll(f[8:], 7, 0)
    return jnp.concatenate([jnp.where(last, r1, r0), jnp.where(last, halo, r1)], axis=0)


def dn_y(f, halo):
    first = row_ids() == 0
    r0, r1 = pltpu.roll(f[:8], 1, 0), pltpu.roll(f[8:], 1, 0)
    return jnp.concatenate([jnp.where(first, halo, r0), jnp.where(first, r0, r1)], axis=0)


def up_i(f):
    return jnp.where(row_ids() == 7, 0.0, pltpu.roll(f, 7, 0))


def dn_i(f):
    return jnp.where(row_ids() == 0, 0.0, pltpu.roll(f, 1, 0))


def only_row(shape, row, value):
    ids = lax.broadcasted_iota(jnp.int32, shape, 0)
    return jnp.where(ids == row, value, 0.0)


def hops(d):
    return min(d, NX4 - d)


def kernel(
    vel_h, str_h, mat_h, bg_h, load_h, slip_h, stat_h, dyn_h, weak_h, seg_h,
    vel_o, str_o, slip_o,
    v, s, m, bg, load, slip, stat, dyn, weak, seg,
    same, coef, face, sn, g,
    xs_lo, xs_hi, ys_lo, ys_hi, cs,
    ixs_lo, ixs_hi, iys_lo, iys_hi,
    xr_lo, xr_hi, yr_lo, yr_hi, cr, ar,
    hx_lo, hx_hi, hy_lo, hy_hi,
    load_sem, send_sem, recv_sem, isend_sem, irecv_sem, out_sem,
):
    gx, gy = lax.axis_index("gx"), lax.axis_index("gy")
    xm, xp = lax.rem(gx + GX - 1, GX), lax.rem(gx + 1, GX)
    ym, yp = lax.rem(gy + GY - 1, GY), lax.rem(gy + 1, GY)
    chip_y, chip_x = gy // NX4, lax.rem(gy, NX4)
    offsets = [(a, b) for a in range(NX4) for b in range(NX4) if a or b]
    offsets.sort(key=lambda o: -(hops(o[0]) + hops(o[1])))
    peers = [
        lax.rem(chip_y + a, NX4) * NX4 + lax.rem(chip_x + b, NX4) for a, b in offsets
    ]

    barrier = pltpu.get_barrier_semaphore()
    others = [(xm, gy), (xp, gy), (xm, ym), (xp, yp), (xp, ym), (xm, yp)]
    greet = [(gx, peer) for peer in peers] + others
    for dev in greet:
        pl.semaphore_signal(barrier, inc=1, device_id=dev, device_id_type=MESH)

    loads = [
        (seg_h.at[0], seg), (stat_h, stat), (dyn_h, dyn), (weak_h, weak),
        (slip_h.at[0], slip), (load_h.at[0], load), (bg_h.at[:, 0], bg),
        (mat_h, m), (str_h, s), (vel_h, v),
    ]
    copies = [
        pltpu.make_async_copy(src, dst, load_sem.at[i]) for i, (src, dst) in enumerate(loads)
    ]
    for copy in copies:
        copy.start()

    copies[0].wait()
    table = seg[...]

    def block_of(lane):
        c = lax.rem(lane, BLOCKS)
        return lane - c + 2 * lax.rem(c, NY) + c // NY

    lane_all = block_of(lax.broadcasted_iota(jnp.int32, (SEGS, TOTAL), 1))
    c = lane_ids(SEGS)
    own_block = jnp.where(c < BLOCKS, gy * BLOCKS + block_of(c), -1)
    member = jnp.zeros((SEGS, TOTAL), jnp.float32)
    own = jnp.zeros((SEGS, LANES), jnp.float32)
    for entry in range(MAXB):
        ids = table[:, entry : entry + 1]
        member = jnp.where(ids == lane_all, 1.0, member)
        own = jnp.where(ids == own_block, 1.0, own)
    own_t = own.T[:BLOCKS]
    shared = jnp.dot(own_t, member, preferred_element_type=jnp.float32)
    same[...] = shared
    count = jnp.sum(shared, axis=1, keepdims=True)
    for copy in copies[1:]:
        copy.wait()
    stat_b = jnp.sum(own_t * stat[...], axis=1, keepdims=True)
    dyn_b = jnp.sum(own_t * dyn[...], axis=1, keepdims=True)
    weak_b = jnp.sum(own_t * weak[...], axis=1, keepdims=True)
    wide = (BLOCKS, LANES)
    coef[0] = jnp.broadcast_to(-1.0 / (LANES * count * weak_b), wide)
    coef[1] = jnp.broadcast_to(stat_b - dyn_b, wide)
    coef[2] = jnp.broadcast_to(dyn_b, wide)

    face[0] = nodes(bg[0])
    face[1] = nodes(bg[1])
    face[2] = nodes(load[...])
    face[3] = 1.0 / nodes(m[1, 0])
    sn[...] = nodes(slip[...])
    for i in range(CX):
        for k in range(3):
            m[k, i] = m[k, i] * DT
        for k, (field, row) in enumerate(
            [(3, 0), (5, 0), (1, 0), (0, 15), (3, 15), (4, 15), (5, 15), (2, 15), (1, 15)]
        ):
            g[k, i : i + 1] = s[field, i, row : row + 1]

    ixs_lo[0], ixs_lo[1] = m[2, 0], v[0, 0]
    ixs_hi[0], ixs_hi[1], ixs_hi[2] = m[2, 7], v[1, 7], v[2, 7]
    for i in range(CX):
        iys_lo[0, i : i + 1], iys_lo[1, i : i + 1] = m[2, i, 0:1], v[1, i, 0:1]
        iys_hi[0, i : i + 1], iys_hi[1, i : i + 1] = m[2, i, 15:16], v[0, i, 15:16]
        iys_hi[2, i : i + 1] = v[2, i, 15:16]

    def remote(src, dst, send, recv, dev):
        return pltpu.make_async_remote_copy(
            src_ref=src, dst_ref=dst, send_sem=send, recv_sem=recv,
            device_id=dev, device_id_type=MESH,
        )

    def once_copies():
        return [
            remote(ixs_lo, hx_hi, isend_sem.at[0], irecv_sem.at[0], (xm, gy)),
            remote(ixs_hi, hx_lo, isend_sem.at[1], irecv_sem.at[1], (xp, gy)),
            remote(iys_lo, hy_hi, isend_sem.at[2], irecv_sem.at[2], (gx, ym)),
            remote(iys_hi, hy_lo, isend_sem.at[3], irecv_sem.at[3], (gx, yp)),
        ]

    def halo_copies(slot):
        def at(kind):
            return send_sem.at[kind], recv_sem.at[kind, slot]

        return {
            XLO: remote(xs_lo, xr_hi.at[slot], *at(XLO), (xm, gy)),
            XHI: remote(xs_hi, xr_lo.at[slot], *at(XHI), (xp, gy)),
            YLO: remote(ys_lo, yr_hi.at[slot], *at(YLO), (gx, ym)),
            YHI: remote(ys_hi, yr_lo.at[slot], *at(YHI), (gx, yp)),
            C0: remote(cs.at[pl.ds(0, 1)], cr.at[slot, pl.ds(0, 1)], *at(C0), (xm, ym)),
            C1: remote(cs.at[pl.ds(1, 2)], cr.at[slot, pl.ds(1, 2)], *at(C1), (xp, yp)),
            C2: remote(cs.at[pl.ds(3, 1)], cr.at[slot, pl.ds(3, 1)], *at(C2), (xp, ym)),
            C3: remote(cs.at[pl.ds(4, 1)], cr.at[slot, pl.ds(4, 1)], *at(C3), (xm, yp)),
        }

    def sums_wait(slot, sem):
        part = ar.at[slot, pl.ds(0, GY - 1)]
        pltpu.make_async_copy(part, part, sem).wait()

    block_lane = lax.rem(gy, 4) * BLOCKS + lax.broadcasted_iota(jnp.int32, wide, 0)
    place = block_lane == lane_ids(BLOCKS)

    def send_sums(slot, slip_now):
        sums = jnp.sum(slip_now, axis=1, keepdims=True)
        row = jnp.sum(jnp.where(place, sums, 0.0), axis=0, keepdims=True)
        ar[slot, gy] = row
        for peer in peers:
            remote(
                ar.at[slot, gy], ar.at[slot, gy],
                send_sem.at[SUMS], recv_sem.at[SUMS, slot], (gx, peer),
            ).start()

    def stage(slot):
        cs[0] = s[3, 0, 0:1]
        cs[1] = s[0, 7, 15:16]
        cs[2] = s[1, 7, 15:16]
        cs[3] = s[5, 7, 0:1]
        cs[4] = s[4, 0, 15:16]
        copies = halo_copies(slot)
        for kind in (C0, C1, C2, C3):
            copies[kind].start()
        g0, g1, g4, g5, g7 = g[0], g[1], g[4], g[5], g[7]
        ys_lo[0] = g0
        ys_lo[1] = g1
        ys_lo[2] = up_i(g0) - g0 + g[2] + (up_z(g1) - g1)
        copies[YLO].start()
        ys_hi[0] = g[8]
        ys_hi[1] = g[3] - dn_i(g[3]) - g4 + (up_z(g5) - g5)
        ys_hi[2] = up_i(g5) - g5 - g[6] + (g7 - dn_z(g7))
        copies[YHI].start()
        xy, xz = s[3, 0], s[4, 0]
        xs_lo[0] = xy
        xs_lo[1] = xz
        xs_lo[2] = s[0, 0] + (up_y(xy, 0.0) - xy) + (up_z(xz) - xz)
        copies[XLO].start()
        yy, zz, yz = s[1, 7], s[2, 7], s[5, 7]
        xs_hi[0] = s[0, 7]
        xs_hi[1] = (yy - dn_y(yy, 0.0)) - s[3, 7] + (up_z(yz) - yz)
        xs_hi[2] = (up_y(yz, 0.0) - yz) - s[4, 7] + (zz - dn_z(zz))
        copies[XHI].start()

    pl.semaphore_wait(barrier, len(greet))
    send_sums(0, sn[...])
    for copy in once_copies():
        copy.start()
    stage(0)
    for copy in once_copies():
        copy.wait_recv()

    def advance(t, carry):
        arriving = halo_copies(t)
        for kind in (XLO, XHI, YLO, YHI, C0, C1, C2, C3):
            arriving[kind].wait_recv()

        tall, flat = (NY, NZ), (CX, NZ)
        corner = [cr[t, k] for k in range(5)]
        acc = xr_hi[t, 2] - s[0, 7] + only_row(tall, 15, corner[0])
        vx_xp = hx_hi[1] + hx_hi[0] * acc
        hx_hi[1] = vx_xp
        acc = xr_lo[t, 1] + s[3, 0] - only_row(tall, 0, corner[2])
        vy_xm = hx_lo[1] + hx_lo[0] * acc
        hx_lo[1] = vy_xm
        acc = xr_lo[t, 2] + s[4, 0] + only_row(tall, 15, corner[3])
        vz_xm = hx_lo[2] + hx_lo[0] * acc
        hx_lo[2] = vz_xm
        acc = yr_lo[t, 1] + g[0] - only_row(flat, 0, corner[1])
        hy_lo[1] = hy_lo[1] + hy_lo[0] * acc
        acc = yr_lo[t, 2] + g[1] + only_row(flat, 7, corner[4])
        hy_lo[2] = hy_lo[2] + hy_lo[0] * acc
        acc = yr_hi[t, 2] - g[8] + only_row(flat, 7, corner[0])
        hy_hi[1] = hy_hi[1] + hy_hi[0] * acc

        for i in range(CX):
            b = m[2, i]
            row = slice(i, i + 1)
            xx_m = s[0, i - 1] if i else xr_lo[t, 0]
            xy_p = s[3, i + 1] if i < CX - 1 else xr_hi[t, 0]
            xz_p = s[4, i + 1] if i < CX - 1 else xr_hi[t, 1]
            xx, yy, zz, xy, xz, yz = (s[k, i] for k in range(6))
            v[0, i] = v[0, i] + b * (
                (xx - xx_m) + (up_y(xy, yr_hi[t, 0, row]) - xy) + (up_z(xz) - xz)
            )
            v[1, i] = v[1, i] + b * (
                (xy_p - xy) + (yy - dn_y(yy, yr_lo[t, 0, row])) + (up_z(yz) - yz)
            )
            v[2, i] = v[2, i] + b * (
                (xz_p - xz) + (up_y(yz, yr_hi[t, 1, row]) - yz) + (zz - dn_z(zz))
            )

        for i in range(CX):
            lam, mu = m[0, i], m[1, i]
            row = slice(i, i + 1)
            vx, vy, vz = v[0, i], v[1, i], v[2, i]
            vx_p = v[0, i + 1] if i < CX - 1 else vx_xp
            vy_m = v[1, i - 1] if i else vy_xm
            vz_m = v[2, i - 1] if i else vz_xm
            ex = vx_p - vx
            ey = up_y(vy, hy_hi[1, row]) - vy
            ez = up_z(vz) - vz
            bulk = lam * (ex + ey + ez)
            mu2 = mu + mu
            xx = s[0, i] + (bulk + mu2 * ex)
            yy = s[1, i] + (bulk + mu2 * ey)
            zz = s[2, i] + (bulk + mu2 * ez)
            xy = s[3, i] + mu * ((vy - vy_m) + (vx - dn_y(vx, hy_lo[1, row])))
            xz = s[4, i] + mu * ((vz - vz_m) + (vx - dn_z(vx)))
            yz = s[5, i] + mu * ((vz - dn_y(vz, hy_lo[2, row])) + (vy - dn_z(vy)))
            for k, field in enumerate((xx, yy, zz, xy, xz, yz)):
                s[k, i] = field
            for k, line in enumerate(
                (xy[0:1], yz[0:1], yy[0:1], xx[15:], xy[15:], xz[15:], yz[15:], zz[15:], yy[15:])
            ):
                g[k, row] = line

        trial_y = nodes(s[3, 0]) + face[0]
        trial_z = nodes(s[4, 0]) + face[1]
        mag = jnp.sqrt(trial_y * trial_y + trial_z * trial_z)
        load_ratio = face[2] / mag
        rate = mag * face[3]
        sums_wait(t, recv_sem.at[SUMS, t])
        total = jnp.zeros(wide, jnp.float32)
        for q in range(4):
            part = ar[t, 4 * q] + ar[t, 4 * q + 1] + ar[t, 4 * q + 2] + ar[t, 4 * q + 3]
            total = total + same[:, q * LANES : (q + 1) * LANES] * part
        seg_sum = jnp.sum(total, axis=1, keepdims=True)
        friction = coef[2] + coef[1] * jnp.exp(seg_sum * coef[0])
        excess = 1.0 - jnp.minimum(friction * load_ratio, 1.0)
        slip_now = sn[...] + rate * excess
        sn[...] = slip_now

        @pl.when(t < STEPS - 1)
        def _():
            sums_wait(t, send_sem.at[SUMS])
            send_sums(t + 1, slip_now)

        xy = s[3, 0] - face_of(trial_y * excess)
        xz = s[4, 0] - face_of(trial_z * excess)
        s[3, 0] = xy
        s[4, 0] = xz
        g[0, 0:1], g[4, 0:1], g[5, 0:1] = xy[0:1], xy[15:], xz[15:]

        @pl.when(t < STEPS - 1)
        def _():
            left = halo_copies(t)
            for kind in (XLO, XHI, YLO, YHI, C0, C1, C2, C3):
                left[kind].wait_send()
            stage(t + 1)

        return carry

    lax.fori_loop(0, STEPS, advance, 0)

    last = halo_copies(STEPS - 1)
    slip[...] = face_of(sn[...])
    outs = [
        pltpu.make_async_copy(v, vel_o, out_sem.at[0]),
        pltpu.make_async_copy(s, str_o, out_sem.at[1]),
        pltpu.make_async_copy(slip, slip_o.at[0], out_sem.at[2]),
    ]
    for copy in outs:
        copy.start()
    for kind in (XLO, XHI, YLO, YHI, C0, C1, C2, C3):
        last[kind].wait_send()
    sums_wait(STEPS - 1, send_sem.at[SUMS])
    for copy in once_copies():
        copy.wait_send()
    for copy in outs:
        copy.wait()


def on_device(*args):
    f32 = jnp.float32
    vm = pltpu.VMEM
    block = (CX, NY, NZ)
    scratch = [
        vm((3, *block), f32), vm((6, *block), f32), vm((3, *block), f32),
        vm((2, NY, NZ), f32), vm((NY, NZ), f32), vm((NY, NZ), f32),
        vm((1, SEGS), f32), vm((1, SEGS), f32), vm((1, SEGS), f32),
        vm((SEGS, MAXB), jnp.int32),
        vm((BLOCKS, TOTAL), f32), vm((3, BLOCKS, LANES), f32), vm((4, BLOCKS, LANES), f32),
        vm((BLOCKS, LANES), f32), vm((9, CX, NZ), f32),
        vm((3, NY, NZ), f32), vm((3, NY, NZ), f32), vm((3, CX, NZ), f32), vm((3, CX, NZ), f32),
        vm((5, 1, NZ), f32),
        vm((2, NY, NZ), f32), vm((3, NY, NZ), f32), vm((2, CX, NZ), f32), vm((3, CX, NZ), f32),
        vm((STEPS, 3, NY, NZ), f32), vm((STEPS, 3, NY, NZ), f32),
        vm((STEPS, 3, CX, NZ), f32), vm((STEPS, 3, CX, NZ), f32),
        vm((STEPS, 5, 1, NZ), f32), vm((STEPS, GY, 1, LANES), f32),
        vm((3, NY, NZ), f32), vm((2, NY, NZ), f32), vm((3, CX, NZ), f32), vm((2, CX, NZ), f32),
        pltpu.SemaphoreType.DMA((10,)), pltpu.SemaphoreType.DMA((9,)),
        pltpu.SemaphoreType.DMA((9, STEPS)), pltpu.SemaphoreType.DMA((4,)),
        pltpu.SemaphoreType.DMA((4,)), pltpu.SemaphoreType.DMA((3,)),
    ]
    anywhere = pl.BlockSpec(memory_space=pl.ANY)
    return pl.pallas_call(
        kernel,
        out_shape=(
            jax.ShapeDtypeStruct((3, *block), f32),
            jax.ShapeDtypeStruct((6, *block), f32),
            jax.ShapeDtypeStruct((1, NY, NZ), f32),
        ),
        in_specs=[anywhere] * 10,
        out_specs=(anywhere,) * 3,
        scratch_shapes=scratch,
        compiler_params=pltpu.CompilerParams(collective_id=0, has_side_effects=True),
        name="fault_steps",
    )(*args)


def solution(mesh):
    wave = P(None, "gx", "gy", None)
    fault = P("gx", "gy", None)
    row = P("gx", None)
    return jax.shard_map(
        on_device,
        mesh=mesh,
        in_specs=(wave, wave, wave, wave, fault, fault, row, row, row, P("gx", None, None)),
        out_specs=(wave, wave, fault),
        check_vma=False,
    )
```

```python
import jax
import jax.numpy as jnp
from jax import lax
from jax.experimental import pallas as pl
from jax.experimental.pallas import tpu as pltpu
from jax.sharding import PartitionSpec as P

STEPS = 16
DT = 0.1
GX, GY, NX4 = 8, 16, 4
CX, NY, NZ = 8, 16, 256
LANES = 128
BLOCKS = NY * NZ // LANES
TOTAL = BLOCKS * GY
SEGS, MAXB = 32, 63
MESH = pl.DeviceIdType.MESH

XHI, YLO, YHI, C1, C2, XLO, LLO, LHI, C0, C3, SUMS = range(11)
EARLY, LATE = (XHI, YLO, YHI, C1, C2), (XLO, LLO, LHI, C0, C3)
SLOTS = 2


def nodes(face):
    return jnp.concatenate([face[:, :LANES], face[:, LANES:]], axis=0)


def face_of(rows):
    return jnp.concatenate([rows[:NY], rows[NY:]], axis=1)


def lane_ids(rows):
    return lax.broadcasted_iota(jnp.int32, (rows, LANES), 1)


def up_z(f):
    lane = lane_ids(f.shape[0])
    a, b = f[:, :LANES], f[:, LANES:]
    ra, rb = pltpu.roll(a, LANES - 1, 1), pltpu.roll(b, LANES - 1, 1)
    last = lane == LANES - 1
    return jnp.concatenate([jnp.where(last, rb, ra), jnp.where(last, 0.0, rb)], axis=1)


def dn_z(f):
    lane = lane_ids(f.shape[0])
    a, b = f[:, :LANES], f[:, LANES:]
    ra, rb = pltpu.roll(a, 1, 1), pltpu.roll(b, 1, 1)
    first = lane == 0
    return jnp.concatenate([jnp.where(first, 0.0, ra), jnp.where(first, ra, rb)], axis=1)


def row_ids():
    return lax.broadcasted_iota(jnp.int32, (8, NZ), 0)


def up_y(f, halo):
    last = row_ids() == 7
    r0, r1 = pltpu.roll(f[:8], 7, 0), pltpu.roll(f[8:], 7, 0)
    return jnp.concatenate([jnp.where(last, r1, r0), jnp.where(last, halo, r1)], axis=0)


def dn_y(f, halo):
    first = row_ids() == 0
    r0, r1 = pltpu.roll(f[:8], 1, 0), pltpu.roll(f[8:], 1, 0)
    return jnp.concatenate([jnp.where(first, halo, r0), jnp.where(first, r0, r1)], axis=0)


def up_i(f):
    return jnp.where(row_ids() == 7, 0.0, pltpu.roll(f, 7, 0))


def dn_i(f):
    return jnp.where(row_ids() == 0, 0.0, pltpu.roll(f, 1, 0))


def only_row(shape, row, value):
    ids = lax.broadcasted_iota(jnp.int32, shape, 0)
    return jnp.where(ids == row, value, 0.0)


def hops(d):
    return min(d, NX4 - d)


def kernel(
    vel_h, str_h, mat_h, bg_h, load_h, slip_h, stat_h, dyn_h, weak_h, seg_h,
    v, s, slip_o,
    m, bg, load, slip, stat, dyn, weak, seg,
    same, coef, face, sn, g,
    xs_lo, xs_hi, ys_lo, ys_hi, ls_lo, ls_hi, cs,
    ixs_lo, ixs_hi, iys_lo, iys_hi,
    xr_lo, xr_hi, yr_lo, yr_hi, lr_lo, lr_hi, cr, ar,
    hx_lo, hx_hi, hy_lo, hy_hi,
    load_sem, send_sem, recv_sem, isend_sem, irecv_sem,
):
    gx, gy = lax.axis_index("gx"), lax.axis_index("gy")
    xm, xp = lax.rem(gx + GX - 1, GX), lax.rem(gx + 1, GX)
    ym, yp = lax.rem(gy + GY - 1, GY), lax.rem(gy + 1, GY)
    chip_y, chip_x = gy // NX4, lax.rem(gy, NX4)
    offsets = [(a, b) for a in range(NX4) for b in range(NX4) if a or b]
    offsets.sort(key=lambda o: -(hops(o[0]) + hops(o[1])))
    peers = [
        lax.rem(chip_y + a, NX4) * NX4 + lax.rem(chip_x + b, NX4) for a, b in offsets
    ]

    barrier = pltpu.get_barrier_semaphore()
    others = [(xm, gy), (xp, gy), (xm, ym), (xp, yp), (xp, ym), (xm, yp)]
    greet = [(gx, peer) for peer in peers] + others
    for dev in greet:
        pl.semaphore_signal(barrier, inc=1, device_id=dev, device_id_type=MESH)

    loads = [
        (seg_h.at[0], seg), (stat_h, stat), (dyn_h, dyn), (weak_h, weak),
        (slip_h.at[0], slip), (load_h.at[0], load), (bg_h.at[:, 0], bg),
        (mat_h, m), (str_h, s), (vel_h, v),
    ]
    copies = [
        pltpu.make_async_copy(src, dst, load_sem.at[i]) for i, (src, dst) in enumerate(loads)
    ]
    for copy in copies:
        copy.start()

    copies[0].wait()
    table = seg[...]

    def block_of(lane):
        c = lax.rem(lane, BLOCKS)
        return lane - c + 2 * lax.rem(c, NY) + c // NY

    lane_all = block_of(lax.broadcasted_iota(jnp.int32, (SEGS, TOTAL), 1))
    c = lane_ids(SEGS)
    own_block = jnp.where(c < BLOCKS, gy * BLOCKS + block_of(c), -1)
    member = jnp.zeros((SEGS, TOTAL), jnp.float32)
    own = jnp.zeros((SEGS, LANES), jnp.float32)
    for entry in range(MAXB):
        ids = table[:, entry : entry + 1]
        member = jnp.where(ids == lane_all, 1.0, member)
        own = jnp.where(ids == own_block, 1.0, own)
    own_t = own.T[:BLOCKS]
    shared = jnp.dot(own_t, member, preferred_element_type=jnp.float32)
    same[...] = shared
    count = jnp.sum(shared, axis=1, keepdims=True)
    for copy in copies[1:]:
        copy.wait()
    stat_b = jnp.sum(own_t * stat[...], axis=1, keepdims=True)
    dyn_b = jnp.sum(own_t * dyn[...], axis=1, keepdims=True)
    weak_b = jnp.sum(own_t * weak[...], axis=1, keepdims=True)
    wide = (BLOCKS, LANES)
    coef[0] = jnp.broadcast_to(-1.0 / (LANES * count * weak_b), wide)
    coef[1] = jnp.broadcast_to(stat_b - dyn_b, wide)
    coef[2] = jnp.broadcast_to(dyn_b, wide)

    face[0] = nodes(bg[0])
    face[1] = nodes(bg[1])
    face[2] = nodes(load[...])
    face[3] = 1.0 / nodes(m[1, 0])
    sn[...] = nodes(slip[...])
    for i in range(CX):
        for k in range(3):
            m[k, i] = m[k, i] * DT
        for k, (field, row) in enumerate(
            [(3, 0), (5, 0), (1, 0), (0, 15), (3, 15), (4, 15), (5, 15), (2, 15), (1, 15)]
        ):
            g[0, k, i : i + 1] = s[field, i, row : row + 1]

    ixs_lo[0], ixs_lo[1] = m[2, 0], v[0, 0]
    ixs_hi[0], ixs_hi[1], ixs_hi[2] = m[2, 7], v[1, 7], v[2, 7]
    for i in range(CX):
        iys_lo[0, i : i + 1], iys_lo[1, i : i + 1] = m[2, i, 0:1], v[1, i, 0:1]
        iys_hi[0, i : i + 1], iys_hi[1, i : i + 1] = m[2, i, 15:16], v[0, i, 15:16]
        iys_hi[2, i : i + 1] = v[2, i, 15:16]

    def remote(src, dst, send, recv, dev):
        return pltpu.make_async_remote_copy(
            src_ref=src, dst_ref=dst, send_sem=send, recv_sem=recv,
            device_id=dev, device_id_type=MESH,
        )

    def once_copies():
        return [
            remote(ixs_lo, hx_hi, isend_sem.at[0], irecv_sem.at[0], (xm, gy)),
            remote(ixs_hi, hx_lo, isend_sem.at[1], irecv_sem.at[1], (xp, gy)),
            remote(iys_lo, hy_hi, isend_sem.at[2], irecv_sem.at[2], (gx, ym)),
            remote(iys_hi, hy_lo, isend_sem.at[3], irecv_sem.at[3], (gx, yp)),
        ]

    def halo(kind, slot):
        def corner(first, size):
            return cs.at[pl.ds(first, size)], cr.at[slot, pl.ds(first, size)]

        src, dst, dev = {
            XHI: lambda: (xs_hi, xr_lo.at[slot], (xp, gy)),
            YLO: lambda: (ys_lo, yr_hi.at[slot], (gx, ym)),
            YHI: lambda: (ys_hi, yr_lo.at[slot], (gx, yp)),
            C1: lambda: (*corner(1, 2), (xp, yp)),
            C2: lambda: (*corner(3, 1), (xp, ym)),
            XLO: lambda: (xs_lo, xr_hi.at[slot], (xm, gy)),
            LLO: lambda: (ls_lo, lr_hi.at[slot], (gx, ym)),
            LHI: lambda: (ls_hi, lr_lo.at[slot], (gx, yp)),
            C0: lambda: (*corner(0, 1), (xm, ym)),
            C3: lambda: (*corner(4, 1), (xm, yp)),
        }[kind]()
        return remote(src, dst, send_sem.at[kind], recv_sem.at[kind, slot], dev)

    def sums_wait(slot, sem):
        part = ar.at[slot, pl.ds(0, GY - 1)]
        pltpu.make_async_copy(part, part, sem).wait()

    block_lane = lax.rem(gy, 4) * BLOCKS + lax.broadcasted_iota(jnp.int32, wide, 0)
    place = block_lane == lane_ids(BLOCKS)

    def send_sums(slot, slip_now):
        sums = jnp.sum(slip_now, axis=1, keepdims=True)
        row = jnp.sum(jnp.where(place, sums, 0.0), axis=0, keepdims=True)
        ar[slot, gy] = row
        for peer in peers:
            remote(
                ar.at[slot, gy], ar.at[slot, gy],
                send_sem.at[SUMS], recv_sem.at[SUMS, slot], (gx, peer),
            ).start()

    def lines(edge):
        g0, g1, g4, g5, g7 = (g[edge, k] for k in (0, 1, 4, 5, 7))
        to_lo = up_i(g0) - g0 + g[edge, 2] + (up_z(g1) - g1)
        to_hi_x = g[edge, 3] - dn_i(g[edge, 3]) - g4 + (up_z(g5) - g5)
        to_hi_z = up_i(g5) - g5 - g[edge, 6] + (g7 - dn_z(g7))
        return to_lo, to_hi_x, to_hi_z

    def send_early(slot):
        cs[1] = s[0, 7, 15:16]
        cs[2] = s[1, 7, 15:16]
        cs[3] = s[5, 7, 0:1]
        halo(C1, slot).start()
        halo(C2, slot).start()
        to_lo, to_hi_x, to_hi_z = lines(slot)
        ys_lo[0], ys_lo[1], ys_lo[2] = g[slot, 0], g[slot, 1], to_lo
        halo(YLO, slot).start()
        ys_hi[0], ys_hi[1], ys_hi[2] = g[slot, 8], to_hi_x, to_hi_z
        halo(YHI, slot).start()
        yy, zz, yz = s[1, 7], s[2, 7], s[5, 7]
        xs_hi[0] = s[0, 7]
        xs_hi[1] = (yy - dn_y(yy, 0.0)) - s[3, 7] + (up_z(yz) - yz)
        xs_hi[2] = (up_y(yz, 0.0) - yz) - s[4, 7] + (zz - dn_z(zz))
        halo(XHI, slot).start()

    def send_late(slot, xy, xz, slip_now):
        cs[0] = xy[0:1]
        cs[4] = xz[15:]
        halo(C0, slot).start()
        halo(C3, slot).start()
        to_lo, to_hi_x, to_hi_z = lines(slot)
        ls_lo[0], ls_lo[1], ls_lo[2] = g[slot, 0, 0:1], g[slot, 1, 0:1], to_lo[0:1]
        halo(LLO, slot).start()
        ls_hi[0], ls_hi[1], ls_hi[2] = g[slot, 8, 0:1], to_hi_x[0:1], to_hi_z[0:1]
        halo(LHI, slot).start()
        send_sums(slot, slip_now)
        xs_lo[0] = xy
        xs_lo[1] = xz
        xs_lo[2] = s[0, 0] + (up_y(xy, 0.0) - xy) + (up_z(xz) - xz)
        halo(XLO, slot).start()

    pl.semaphore_wait(barrier, len(greet))
    for copy in once_copies():
        copy.start()
    send_late(0, s[3, 0], s[4, 0], sn[...])
    send_early(0)
    for copy in once_copies():
        copy.wait_recv()

    tall, flat = (NY, NZ), (CX, NZ)

    def advance(t, carry):
        now, later = lax.rem(t, SLOTS), lax.rem(t + 1, SLOTS)

        def own_velocity(i, comps, up_line, down_line, up_line_z):
            b = m[2, i]
            xx, yy, zz, xy, xz, yz = (s[k, i] for k in range(6))
            if 0 in comps:
                xx_m = s[0, i - 1] if i else xr_lo[now, 0]
                v[0, i] = v[0, i] + b * ((xx - xx_m) + (up_y(xy, up_line) - xy) + (up_z(xz) - xz))
            if 1 in comps:
                xy_p = s[3, i + 1] if i < CX - 1 else xr_hi[now, 0]
                v[1, i] = v[1, i] + b * ((xy_p - xy) + (yy - dn_y(yy, down_line)) + (up_z(yz) - yz))
            if 2 in comps:
                xz_p = s[4, i + 1] if i < CX - 1 else xr_hi[now, 1]
                v[2, i] = v[2, i] + b * ((xz_p - xz) + (up_y(yz, up_line_z) - yz) + (zz - dn_z(zz)))

        def own_stress(i, vx_p, vy_m, vz_m):
            lam, mu = m[0, i], m[1, i]
            row = slice(i, i + 1)
            vx, vy, vz = v[0, i], v[1, i], v[2, i]
            ex = vx_p - vx
            ey = up_y(vy, hy_hi[1, row]) - vy
            ez = up_z(vz) - vz
            bulk = lam * (ex + ey + ez)
            mu2 = mu + mu
            xx = s[0, i] + (bulk + mu2 * ex)
            yy = s[1, i] + (bulk + mu2 * ey)
            zz = s[2, i] + (bulk + mu2 * ez)
            xy = s[3, i] + mu * ((vy - vy_m) + (vx - dn_y(vx, hy_lo[1, row])))
            xz = s[4, i] + mu * ((vz - vz_m) + (vx - dn_z(vx)))
            yz = s[5, i] + mu * ((vz - dn_y(vz, hy_lo[2, row])) + (vy - dn_z(vy)))
            for k, field in enumerate((xx, yy, zz, xy, xz, yz)):
                s[k, i] = field
            for k, line in enumerate(
                (xy[0:1], yz[0:1], yy[0:1], xx[15:], xy[15:], xz[15:], yz[15:], zz[15:], yy[15:])
            ):
                g[later, k, row] = line
            return xy, xz

        for i in range(1, CX):
            own_velocity(i, (0, 1, 2) if i < CX - 1 else (0,), 0.0, 0.0, 0.0)

        for kind in (YLO, YHI):
            halo(kind, now).wait_recv()
        inner = row_ids() > 0
        first, last = row_ids() == 0, row_ids() == 7
        acc = yr_lo[now, 1] + g[now, 0]
        hy_lo[1] = hy_lo[1] + hy_lo[0] * jnp.where(inner, acc, 0.0)
        acc = yr_lo[now, 2] + g[now, 1]
        hy_lo[2] = hy_lo[2] + hy_lo[0] * jnp.where(inner, acc, 0.0)
        acc = yr_hi[now, 2] - g[now, 8]
        hy_hi[1] = hy_hi[1] + hy_hi[0] * jnp.where(inner, acc, 0.0)

        def add_lines(i, up_line, down_line, up_line_z):
            if up_line is not None:
                v[0, i, 8:] = v[0, i, 8:] + m[2, i, 8:] * jnp.where(last, up_line, 0.0)
            if down_line is not None:
                v[1, i, :8] = v[1, i, :8] - m[2, i, :8] * jnp.where(first, down_line, 0.0)
                v[2, i, 8:] = v[2, i, 8:] + m[2, i, 8:] * jnp.where(last, up_line_z, 0.0)

        for i in range(1, CX):
            row = slice(i, i + 1)
            if i < CX - 1:
                add_lines(i, yr_hi[now, 0, row], yr_lo[now, 0, row], yr_hi[now, 1, row])
            else:
                add_lines(i, yr_hi[now, 0, row], None, None)
        for i in range(2, CX - 1):
            own_stress(i, v[0, i + 1], v[1, i - 1], v[2, i - 1])

        for kind in (XHI, LLO, LHI, C1, C2):
            halo(kind, now).wait_recv()
        acc = xr_lo[now, 1] + s[3, 0] - only_row(tall, 0, cr[now, 2])
        vy_xm = hx_lo[1] + hx_lo[0] * acc
        hx_lo[1] = vy_xm
        acc = xr_lo[now, 2] + s[4, 0] + only_row(tall, 15, cr[now, 3])
        vz_xm = hx_lo[2] + hx_lo[0] * acc
        hx_lo[2] = vz_xm
        acc = lr_lo[now, 1] + g[now, 0, 0:1] - cr[now, 1]
        hy_lo[1] = hy_lo[1] + hy_lo[0] * only_row(flat, 0, acc)
        acc = lr_lo[now, 2] + g[now, 1, 0:1]
        hy_lo[2] = hy_lo[2] + hy_lo[0] * only_row(flat, 0, acc)
        acc = lr_hi[now, 2] - g[now, 8, 0:1]
        hy_hi[1] = hy_hi[1] + hy_hi[0] * only_row(flat, 0, acc)
        own_velocity(0, (0, 1, 2), lr_hi[now, 0], lr_lo[now, 0], lr_hi[now, 1])
        xy0, xz0 = own_stress(0, v[0, 1], vy_xm, vz_xm)
        own_stress(1, v[0, 2], v[1, 0], v[2, 0])
        trial_y = nodes(xy0) + face[0]
        trial_z = nodes(xz0) + face[1]
        mag = jnp.sqrt(trial_y * trial_y + trial_z * trial_z)
        load_ratio = face[2] / mag
        rate = mag * face[3]

        for kind in (XLO, C0, C3):
            halo(kind, now).wait_recv()
        acc = xr_hi[now, 2] - s[0, 7] + only_row(tall, 15, cr[now, 0])
        vx_xp = hx_hi[1] + hx_hi[0] * acc
        hx_hi[1] = vx_xp
        hy_lo[2] = hy_lo[2] + hy_lo[0] * only_row(flat, 7, cr[now, 4])
        hy_hi[1] = hy_hi[1] + hy_hi[0] * only_row(flat, 7, cr[now, 0])
        row = slice(7, 8)
        own_velocity(7, (1, 2), None, yr_lo[now, 0, row], yr_hi[now, 1, row])
        own_stress(7, vx_xp, v[1, 6], v[2, 6])

        @pl.when(t < STEPS - 1)
        def _():
            for kind in EARLY:
                halo(kind, now).wait_send()
            send_early(later)

        sums_wait(now, recv_sem.at[SUMS, now])
        total = jnp.zeros(wide, jnp.float32)
        for q in range(4):
            part = ar[now, 4 * q] + ar[now, 4 * q + 1] + ar[now, 4 * q + 2] + ar[now, 4 * q + 3]
            total = total + same[:, q * LANES : (q + 1) * LANES] * part
        seg_sum = jnp.sum(total, axis=1, keepdims=True)
        friction = coef[2] + coef[1] * jnp.exp(seg_sum * coef[0])
        excess = 1.0 - jnp.minimum(friction * load_ratio, 1.0)
        slip_now = sn[...] + rate * excess
        sn[...] = slip_now
        xy = xy0 - face_of(trial_y * excess)
        xz = xz0 - face_of(trial_z * excess)
        s[3, 0] = xy
        s[4, 0] = xz

        @pl.when(t < STEPS - 1)
        def _():
            for kind in LATE:
                halo(kind, now).wait_send()
            sums_wait(now, send_sem.at[SUMS])
            g[later, 0, 0:1], g[later, 4, 0:1], g[later, 5, 0:1] = xy[0:1], xy[15:], xz[15:]
            send_late(later, xy, xz, slip_now)

        return carry

    lax.fori_loop(0, STEPS, advance, 0)

    slip_o[0] = face_of(sn[...])
    for kind in EARLY + LATE:
        halo(kind, 0).wait_send()
    sums_wait(0, send_sem.at[SUMS])
    for copy in once_copies():
        copy.wait_send()


def on_device(*args):
    f32 = jnp.float32
    vm = pltpu.VMEM
    block = (CX, NY, NZ)
    scratch = [
        vm((3, *block), f32),
        vm((2, NY, NZ), f32), vm((NY, NZ), f32), vm((NY, NZ), f32),
        vm((1, SEGS), f32), vm((1, SEGS), f32), vm((1, SEGS), f32),
        vm((SEGS, MAXB), jnp.int32),
        vm((BLOCKS, TOTAL), f32), vm((3, BLOCKS, LANES), f32), vm((4, BLOCKS, LANES), f32),
        vm((BLOCKS, LANES), f32), vm((SLOTS, 9, CX, NZ), f32),
        vm((3, NY, NZ), f32), vm((3, NY, NZ), f32), vm((3, CX, NZ), f32), vm((3, CX, NZ), f32),
        vm((3, 1, NZ), f32), vm((3, 1, NZ), f32), vm((5, 1, NZ), f32),
        vm((2, NY, NZ), f32), vm((3, NY, NZ), f32), vm((2, CX, NZ), f32), vm((3, CX, NZ), f32),
        vm((SLOTS, 3, NY, NZ), f32), vm((SLOTS, 3, NY, NZ), f32),
        vm((SLOTS, 3, CX, NZ), f32), vm((SLOTS, 3, CX, NZ), f32),
        vm((SLOTS, 3, 1, NZ), f32), vm((SLOTS, 3, 1, NZ), f32),
        vm((SLOTS, 5, 1, NZ), f32), vm((SLOTS, GY, 1, LANES), f32),
        vm((3, NY, NZ), f32), vm((2, NY, NZ), f32), vm((3, CX, NZ), f32), vm((2, CX, NZ), f32),
        pltpu.SemaphoreType.DMA((10,)), pltpu.SemaphoreType.DMA((11,)),
        pltpu.SemaphoreType.DMA((11, SLOTS)), pltpu.SemaphoreType.DMA((4,)),
        pltpu.SemaphoreType.DMA((4,)),
    ]
    anywhere = pl.BlockSpec(memory_space=pltpu.HBM)
    return pl.pallas_call(
        kernel,
        out_shape=(
            jax.ShapeDtypeStruct((3, *block), f32),
            jax.ShapeDtypeStruct((6, *block), f32),
            jax.ShapeDtypeStruct((1, NY, NZ), f32),
        ),
        in_specs=[anywhere] * 10,
        out_specs=(pl.BlockSpec(memory_space=pltpu.VMEM),) * 3,
        scratch_shapes=scratch,
        compiler_params=pltpu.CompilerParams(
            collective_id=0, has_side_effects=True, vmem_limit_bytes=62 << 20
        ),
        name="fault_steps",
    )(*args)


def solution(mesh):
    wave = P(None, "gx", "gy", None)
    fault = P("gx", "gy", None)
    row = P("gx", None)
    return jax.shard_map(
        on_device,
        mesh=mesh,
        in_specs=(wave, wave, wave, wave, fault, fault, row, row, row, P("gx", None, None)),
        out_specs=(wave, wave, fault),
        check_vma=False,
    )
```

```python
import jax
import jax.numpy as jnp
from jax import lax
from jax.experimental import pallas as pl
from jax.experimental.pallas import tpu as pltpu
from jax.sharding import PartitionSpec as P

STEPS = 16
DT = 0.1
GX, GY, NX4 = 8, 16, 4
CX, NY, NZ = 8, 16, 256
LANES = 128
BLOCKS = NY * NZ // LANES
TOTAL = BLOCKS * GY
SEGS, MAXB = 32, 63
MESH = pl.DeviceIdType.MESH

YLO, YHI, C1, C2, XHI, XLO, LLO, LHI, C0, C3, SUMS = range(11)
EARLY, LATE = (YLO, YHI, C1, C2), (XHI, XLO, LLO, LHI, C0, C3)
LINES = (
    (3, 0), (5, 0), (1, 0), (0, 15), (3, 15), (4, 15), (5, 15), (2, 15), (1, 15), (0, 0), (2, 0)
)
VLINES = ((0, 15), (2, 15), (1, 0))
SLOTS = 2


def nodes(face):
    return jnp.concatenate([face[:, :LANES], face[:, LANES:]], axis=0)


def face_of(rows):
    return jnp.concatenate([rows[:NY], rows[NY:]], axis=1)


def lane_ids(rows):
    return lax.broadcasted_iota(jnp.int32, (rows, LANES), 1)


def up_z(f):
    lane = lane_ids(f.shape[0])
    a, b = f[:, :LANES], f[:, LANES:]
    ra, rb = pltpu.roll(a, LANES - 1, 1), pltpu.roll(b, LANES - 1, 1)
    last = lane == LANES - 1
    return jnp.concatenate([jnp.where(last, rb, ra), jnp.where(last, 0.0, rb)], axis=1)


def dn_z(f):
    lane = lane_ids(f.shape[0])
    a, b = f[:, :LANES], f[:, LANES:]
    ra, rb = pltpu.roll(a, 1, 1), pltpu.roll(b, 1, 1)
    first = lane == 0
    return jnp.concatenate([jnp.where(first, 0.0, ra), jnp.where(first, ra, rb)], axis=1)


def row_ids():
    return lax.broadcasted_iota(jnp.int32, (8, NZ), 0)


def up_y(f, halo):
    last = row_ids() == 7
    r0, r1 = pltpu.roll(f[:8], 7, 0), pltpu.roll(f[8:], 7, 0)
    return jnp.concatenate([jnp.where(last, r1, r0), jnp.where(last, halo, r1)], axis=0)


def dn_y(f, halo):
    first = row_ids() == 0
    r0, r1 = pltpu.roll(f[:8], 1, 0), pltpu.roll(f[8:], 1, 0)
    return jnp.concatenate([jnp.where(first, halo, r0), jnp.where(first, r0, r1)], axis=0)


def up_i(f):
    return jnp.where(row_ids() == 7, 0.0, pltpu.roll(f, 7, 0))


def dn_i(f):
    return jnp.where(row_ids() == 0, 0.0, pltpu.roll(f, 1, 0))


def hops(d):
    return min(d, NX4 - d)


def kernel(
    vel_h, str_h, mat_h, bg_h, load_h, slip_h, stat_h, dyn_h, weak_h, seg_h,
    v, s, slip_o,
    m, bg, load, slip, stat, dyn, weak, seg,
    same, coef, face, sn, g, gv, fm,
    xs_lo, xs_hi, ys_lo, ys_hi, ls_lo, ls_hi, cs,
    ixs_lo, ixs_hi, iys_lo, iys_hi,
    xr_lo, xr_hi, yr_lo, yr_hi, lr_lo, lr_hi, cr, ar,
    hx_lo, hx_hi, hy_lo, hy_hi,
    load_sem, send_sem, recv_sem, isend_sem, irecv_sem,
):
    gx, gy = lax.axis_index("gx"), lax.axis_index("gy")
    xm, xp = lax.rem(gx + GX - 1, GX), lax.rem(gx + 1, GX)
    ym, yp = lax.rem(gy + GY - 1, GY), lax.rem(gy + 1, GY)
    chip_y, chip_x = gy // NX4, lax.rem(gy, NX4)
    offsets = [(a, b) for a in range(NX4) for b in range(NX4) if a or b]
    offsets.sort(key=lambda o: -(hops(o[0]) + hops(o[1])))
    peers = [
        lax.rem(chip_y + a, NX4) * NX4 + lax.rem(chip_x + b, NX4) for a, b in offsets
    ]

    barrier = pltpu.get_barrier_semaphore()
    others = [(xm, gy), (xp, gy), (xm, ym), (xp, yp), (xp, ym), (xm, yp)]
    greet = [(gx, peer) for peer in peers] + others
    for dev in greet:
        pl.semaphore_signal(barrier, inc=1, device_id=dev, device_id_type=MESH)

    loads = [
        (seg_h.at[0], seg), (stat_h, stat), (dyn_h, dyn), (weak_h, weak),
        (slip_h.at[0], slip), (load_h.at[0], load), (bg_h.at[:, 0], bg),
        (mat_h, m), (str_h, s), (vel_h, v),
    ]
    copies = [
        pltpu.make_async_copy(src, dst, load_sem.at[i]) for i, (src, dst) in enumerate(loads)
    ]
    for copy in copies:
        copy.start()

    copies[0].wait()
    table = seg[...]

    def block_of(lane):
        c = lax.rem(lane, BLOCKS)
        return lane - c + 2 * lax.rem(c, NY) + c // NY

    lane_all = block_of(lax.broadcasted_iota(jnp.int32, (SEGS, TOTAL), 1))
    c = lane_ids(SEGS)
    own_block = jnp.where(c < BLOCKS, gy * BLOCKS + block_of(c), -1)
    member = jnp.zeros((SEGS, TOTAL), jnp.float32)
    own = jnp.zeros((SEGS, LANES), jnp.float32)
    for entry in range(MAXB):
        ids = table[:, entry : entry + 1]
        member = jnp.where(ids == lane_all, 1.0, member)
        own = jnp.where(ids == own_block, 1.0, own)
    own_t = own.T[:BLOCKS]
    shared = jnp.dot(own_t, member, preferred_element_type=jnp.float32)
    same[...] = shared
    count = jnp.sum(shared, axis=1, keepdims=True)
    for copy in copies[1:]:
        copy.wait()
    stat_b = jnp.sum(own_t * stat[...], axis=1, keepdims=True)
    dyn_b = jnp.sum(own_t * dyn[...], axis=1, keepdims=True)
    weak_b = jnp.sum(own_t * weak[...], axis=1, keepdims=True)
    wide = (BLOCKS, LANES)
    coef[0] = jnp.broadcast_to(-1.0 / (LANES * count * weak_b), wide)
    coef[1] = jnp.broadcast_to(stat_b - dyn_b, wide)
    coef[2] = jnp.broadcast_to(dyn_b, wide)

    face[0] = nodes(bg[0])
    face[1] = nodes(bg[1])
    face[2] = nodes(load[...])
    face[3] = 1.0 / nodes(m[1, 0])
    sn[...] = nodes(slip[...])
    for i in range(CX):
        for k in range(3):
            m[k, i] = m[k, i] * DT
        for k, (field, row) in enumerate(LINES):
            g[0, k, i : i + 1] = s[field, i, row : row + 1]
        for k in range(3):
            fm[k, 0, i : i + 1] = m[k, i, 0:1]
            fm[k, 1, i : i + 1] = m[k, i, 15:16]

    ixs_lo[0], ixs_lo[1] = m[2, 0], v[0, 0]
    ixs_hi[0], ixs_hi[1], ixs_hi[2] = m[2, 7], v[1, 7], v[2, 7]
    for i in range(CX):
        iys_lo[0, i : i + 1], iys_lo[1, i : i + 1] = m[2, i, 0:1], v[1, i, 0:1]
        iys_hi[0, i : i + 1], iys_hi[1, i : i + 1] = m[2, i, 15:16], v[0, i, 15:16]
        iys_hi[2, i : i + 1] = v[2, i, 15:16]

    def remote(src, dst, send, recv, dev):
        return pltpu.make_async_remote_copy(
            src_ref=src, dst_ref=dst, send_sem=send, recv_sem=recv,
            device_id=dev, device_id_type=MESH,
        )

    def once_copies():
        return [
            remote(ixs_lo, hx_hi, isend_sem.at[0], irecv_sem.at[0], (xm, gy)),
            remote(ixs_hi, hx_lo, isend_sem.at[1], irecv_sem.at[1], (xp, gy)),
            remote(iys_lo, hy_hi, isend_sem.at[2], irecv_sem.at[2], (gx, ym)),
            remote(iys_hi, hy_lo, isend_sem.at[3], irecv_sem.at[3], (gx, yp)),
        ]

    def halo(kind, slot):
        def corner(first, size):
            return cs.at[pl.ds(first, size)], cr.at[slot, pl.ds(first, size)]

        src, dst, dev = {
            XHI: lambda: (xs_hi, xr_lo.at[slot], (xp, gy)),
            YLO: lambda: (ys_lo, yr_hi.at[slot], (gx, ym)),
            YHI: lambda: (ys_hi, yr_lo.at[slot], (gx, yp)),
            C1: lambda: (*corner(1, 2), (xp, yp)),
            C2: lambda: (*corner(3, 1), (xp, ym)),
            XLO: lambda: (xs_lo, xr_hi.at[slot], (xm, gy)),
            LLO: lambda: (ls_lo, lr_hi.at[slot], (gx, ym)),
            LHI: lambda: (ls_hi, lr_lo.at[slot], (gx, yp)),
            C0: lambda: (*corner(0, 1), (xm, ym)),
            C3: lambda: (*corner(4, 1), (xm, yp)),
        }[kind]()
        return remote(src, dst, send_sem.at[kind], recv_sem.at[kind, slot], dev)

    def sums_wait(slot, sem):
        part = ar.at[slot, pl.ds(0, GY - 1)]
        pltpu.make_async_copy(part, part, sem).wait()

    block_lane = lax.rem(gy, 4) * BLOCKS + lax.broadcasted_iota(jnp.int32, wide, 0)
    place = block_lane == lane_ids(BLOCKS)

    def send_sums(slot, slip_now):
        sums = jnp.sum(slip_now, axis=1, keepdims=True)
        row = jnp.sum(jnp.where(place, sums, 0.0), axis=0, keepdims=True)
        ar[slot, gy] = row
        for peer in peers:
            remote(
                ar.at[slot, gy], ar.at[slot, gy],
                send_sem.at[SUMS], recv_sem.at[SUMS, slot], (gx, peer),
            ).start()

    def lines(edge):
        g0, g1, g4, g5, g7 = (g[edge, k] for k in (0, 1, 4, 5, 7))
        to_lo = up_i(g0) - g0 + g[edge, 2] + (up_z(g1) - g1)
        to_hi_x = g[edge, 3] - dn_i(g[edge, 3]) - g4 + (up_z(g5) - g5)
        to_hi_z = up_i(g5) - g5 - g[edge, 6] + (g7 - dn_z(g7))
        return to_lo, to_hi_x, to_hi_z

    def send_early(slot):
        cs[1] = g[slot, 3, 7:8]
        cs[2] = g[slot, 8, 7:8]
        cs[3] = g[slot, 1, 7:8]
        halo(C1, slot).start()
        halo(C2, slot).start()
        to_lo, to_hi_x, to_hi_z = lines(slot)
        ys_lo[0], ys_lo[1], ys_lo[2] = g[slot, 0], g[slot, 1], to_lo
        halo(YLO, slot).start()
        ys_hi[0], ys_hi[1], ys_hi[2] = g[slot, 8], to_hi_x, to_hi_z
        halo(YHI, slot).start()

    def send_late(slot, xy, xz, slip_now):
        cs[0] = xy[0:1]
        cs[4] = xz[15:]
        halo(C0, slot).start()
        halo(C3, slot).start()
        to_lo, to_hi_x, to_hi_z = lines(slot)
        ls_lo[0], ls_lo[1], ls_lo[2] = g[slot, 0, 0:1], g[slot, 1, 0:1], to_lo[0:1]
        halo(LLO, slot).start()
        ls_hi[0], ls_hi[1], ls_hi[2] = g[slot, 8, 0:1], to_hi_x[0:1], to_hi_z[0:1]
        halo(LHI, slot).start()
        send_sums(slot, slip_now)

    def send_rows(slot):
        xy, xz = s[3, 0], s[4, 0]
        xs_lo[0] = xy
        xs_lo[1] = xz
        xs_lo[2] = s[0, 0] + (up_y(xy, 0.0) - xy) + (up_z(xz) - xz)
        halo(XLO, slot).start()
        yy, zz, yz = s[1, 7], s[2, 7], s[5, 7]
        xs_hi[0] = s[0, 7]
        xs_hi[1] = (yy - dn_y(yy, 0.0)) - s[3, 7] + (up_z(yz) - yz)
        xs_hi[2] = (up_y(yz, 0.0) - yz) - s[4, 7] + (zz - dn_z(zz))
        halo(XHI, slot).start()

    pl.semaphore_wait(barrier, len(greet))
    for copy in once_copies():
        copy.start()
    send_early(0)
    send_late(0, s[3, 0], s[4, 0], sn[...])
    send_rows(0)
    for copy in once_copies():
        copy.wait_recv()

    def advance(t, carry):
        now, later = lax.rem(t, SLOTS), lax.rem(t + 1, SLOTS)

        for kind in (XLO, XHI):
            halo(kind, now).wait_recv()
        vx_xp = hx_hi[1] + hx_hi[0] * (xr_hi[now, 2] - s[0, 7])
        vy_xm = hx_lo[1] + hx_lo[0] * (xr_lo[now, 1] + s[3, 0])
        vz_xm = hx_lo[2] + hx_lo[0] * (xr_lo[now, 2] + s[4, 0])
        hx_hi[1], hx_lo[1], hx_lo[2] = vx_xp, vy_xm, vz_xm
        for i in range(CX):
            b = m[2, i]
            row = slice(i, i + 1)
            xx_m = s[0, i - 1] if i else xr_lo[now, 0]
            xy_p = s[3, i + 1] if i < CX - 1 else xr_hi[now, 0]
            xz_p = s[4, i + 1] if i < CX - 1 else xr_hi[now, 1]
            xx, yy, zz, xy, xz, yz = (s[k, i] for k in range(6))
            vx = v[0, i] + b * ((xx - xx_m) + (up_y(xy, 0.0) - xy) + (up_z(xz) - xz))
            vy = v[1, i] + b * ((xy_p - xy) + (yy - dn_y(yy, 0.0)) + (up_z(yz) - yz))
            vz = v[2, i] + b * ((xz_p - xz) + (up_y(yz, 0.0) - yz) + (zz - dn_z(zz)))
            v[0, i], v[1, i], v[2, i] = vx, vy, vz
            gv[0, row], gv[1, row], gv[2, row] = vx[15:], vz[15:], vy[0:1]
        for i in range(CX):
            lam, mu = m[0, i], m[1, i]
            row = slice(i, i + 1)
            vx, vy, vz = v[0, i], v[1, i], v[2, i]
            vx_p = v[0, i + 1] if i < CX - 1 else vx_xp
            vy_m = v[1, i - 1] if i else vy_xm
            vz_m = v[2, i - 1] if i else vz_xm
            ex = vx_p - vx
            ey = up_y(vy, 0.0) - vy
            ez = up_z(vz) - vz
            bulk = lam * (ex + ey + ez)
            mu2 = mu + mu
            fields = (
                s[0, i] + (bulk + mu2 * ex),
                s[1, i] + (bulk + mu2 * ey),
                s[2, i] + (bulk + mu2 * ez),
                s[3, i] + mu * ((vy - vy_m) + (vx - dn_y(vx, 0.0))),
                s[4, i] + mu * ((vz - vz_m) + (vx - dn_z(vx))),
                s[5, i] + mu * ((vz - dn_y(vz, 0.0)) + (vy - dn_z(vy))),
            )
            if i == 0:
                xy_row, xz_row = fields[3], fields[4]
            for k, field in enumerate(fields):
                s[k, i] = field
            for k, (field, line) in enumerate(LINES):
                g[later, k, row] = fields[field][line : line + 1]

        for kind in (YLO, YHI, LLO, LHI, C0, C1, C2, C3):
            halo(kind, now).wait_recv()
        first, last = row_ids() == 0, row_ids() == 7
        up_xy, up_yz, acc_vy = (
            jnp.where(first, lr_hi[now, k], yr_hi[now, k]) for k in range(3)
        )
        dn_yy, acc_vx, acc_vz = (
            jnp.where(first, lr_lo[now, k], yr_lo[now, k]) for k in range(3)
        )
        corner = [cr[now, k] for k in range(5)]
        vx_ym = hy_lo[1] + hy_lo[0] * (acc_vx + g[now, 0] - jnp.where(first, corner[1], 0.0))
        vz_ym = hy_lo[2] + hy_lo[0] * (acc_vz + g[now, 1] + jnp.where(last, corner[4], 0.0))
        vy_yp = hy_hi[1] + hy_hi[0] * (acc_vy - g[now, 8] + jnp.where(last, corner[0], 0.0))
        hy_lo[1], hy_lo[2], hy_hi[1] = vx_ym, vz_ym, vy_yp
        dvx_xp = hx_hi[0, 15:16] * corner[0]
        dvy_xm = -hx_lo[0, 0:1] * corner[2]
        dvz_xm = hx_lo[0, 15:16] * corner[3]
        hx_hi[1, 15:16] = hx_hi[1, 15:16] + dvx_xp
        hx_lo[1, 0:1] = hx_lo[1, 0:1] + dvy_xm
        hx_lo[2, 15:16] = hx_lo[2, 15:16] + dvz_xm
        dvx, dvz, dvy = fm[2, 1] * up_xy, fm[2, 1] * up_yz, -fm[2, 0] * dn_yy
        gv[0], gv[1], gv[2] = gv[0] + dvx, gv[1] + dvz, gv[2] + dvy
        lam, mu = fm[0, 1], fm[1, 1]
        ex = jnp.where(last, dvx_xp, pltpu.roll(dvx, 7, 0)) - dvx
        ez = up_z(dvz) - dvz
        bulk = lam * (ex + vy_yp + ez)
        mu2 = mu + mu
        dvz_m = jnp.where(first, dvz_xm, pltpu.roll(dvz, 1, 0))
        xy15 = g[later, 4] + mu * dvx
        xz15 = g[later, 5] + mu * ((dvz - dvz_m) + (dvx - dn_z(dvx)))
        g[later, 3] = g[later, 3] + (bulk + mu2 * ex)
        g[later, 8] = g[later, 8] + (bulk + mu2 * vy_yp)
        g[later, 7] = g[later, 7] + (bulk + mu2 * ez)
        g[later, 4] = xy15
        g[later, 5] = xz15
        g[later, 6] = g[later, 6] + mu * dvz
        lam, mu = fm[0, 0], fm[1, 0]
        bulk = lam * dvy
        dvy_m = jnp.where(first, dvy_xm, pltpu.roll(dvy, 1, 0))
        xy00 = g[later, 0] + mu * ((dvy - dvy_m) - vx_ym)
        g[later, 9] = g[later, 9] - bulk
        g[later, 10] = g[later, 10] - bulk
        g[later, 2] = g[later, 2] - (bulk + (mu + mu) * dvy)
        g[later, 0] = xy00
        g[later, 1] = g[later, 1] + mu * ((dvy - dn_z(dvy)) - vz_ym)

        @pl.when(t < STEPS - 1)
        def _():
            for kind in EARLY:
                halo(kind, now).wait_send()
            send_early(later)

        def patch(row, line0, line15):
            low = row[:8] if line0 is None else jnp.where(first, line0, row[:8])
            return jnp.concatenate([low, jnp.where(last, line15, row[8:])], axis=0)

        xy0 = patch(xy_row, xy00[0:1], xy15[0:1])
        xz0 = patch(xz_row, None, xz15[0:1])
        trial_y = nodes(xy0) + face[0]
        trial_z = nodes(xz0) + face[1]
        mag = jnp.sqrt(trial_y * trial_y + trial_z * trial_z)
        load_ratio = face[2] / mag
        rate = mag * face[3]

        sums_wait(now, recv_sem.at[SUMS, now])
        total = jnp.zeros(wide, jnp.float32)
        for q in range(4):
            part = ar[now, 4 * q] + ar[now, 4 * q + 1] + ar[now, 4 * q + 2] + ar[now, 4 * q + 3]
            total = total + same[:, q * LANES : (q + 1) * LANES] * part
        seg_sum = jnp.sum(total, axis=1, keepdims=True)
        friction = coef[2] + coef[1] * jnp.exp(seg_sum * coef[0])
        excess = 1.0 - jnp.minimum(friction * load_ratio, 1.0)
        slip_now = sn[...] + rate * excess
        sn[...] = slip_now
        xy = xy0 - face_of(trial_y * excess)
        xz = xz0 - face_of(trial_z * excess)
        s[3, 0] = xy
        s[4, 0] = xz
        g[later, 0, 0:1], g[later, 4, 0:1], g[later, 5, 0:1] = xy[0:1], xy[15:], xz[15:]

        @pl.when(t < STEPS - 1)
        def _():
            for kind in LATE:
                halo(kind, now).wait_send()
            sums_wait(now, send_sem.at[SUMS])
            send_late(later, xy, xz, slip_now)

        for i in range(CX):
            row = slice(i, i + 1)
            for k, (field, line) in enumerate(LINES):
                s[field, i, line : line + 1] = g[later, k, row]
            for k, (field, line) in enumerate(VLINES):
                v[field, i, line : line + 1] = gv[k, row]

        @pl.when(t < STEPS - 1)
        def _():
            send_rows(later)

        return carry

    lax.fori_loop(0, STEPS, advance, 0)

    slip_o[0] = face_of(sn[...])
    for kind in EARLY + LATE:
        halo(kind, 0).wait_send()
    sums_wait(0, send_sem.at[SUMS])
    for copy in once_copies():
        copy.wait_send()


def on_device(*args):
    f32 = jnp.float32
    vm = pltpu.VMEM
    block = (CX, NY, NZ)
    scratch = [
        vm((3, *block), f32),
        vm((2, NY, NZ), f32), vm((NY, NZ), f32), vm((NY, NZ), f32),
        vm((1, SEGS), f32), vm((1, SEGS), f32), vm((1, SEGS), f32),
        vm((SEGS, MAXB), jnp.int32),
        vm((BLOCKS, TOTAL), f32), vm((3, BLOCKS, LANES), f32), vm((4, BLOCKS, LANES), f32),
        vm((BLOCKS, LANES), f32), vm((SLOTS, len(LINES), CX, NZ), f32),
        vm((3, CX, NZ), f32), vm((3, 2, CX, NZ), f32),
        vm((3, NY, NZ), f32), vm((3, NY, NZ), f32), vm((3, CX, NZ), f32), vm((3, CX, NZ), f32),
        vm((3, 1, NZ), f32), vm((3, 1, NZ), f32), vm((5, 1, NZ), f32),
        vm((2, NY, NZ), f32), vm((3, NY, NZ), f32), vm((2, CX, NZ), f32), vm((3, CX, NZ), f32),
        vm((SLOTS, 3, NY, NZ), f32), vm((SLOTS, 3, NY, NZ), f32),
        vm((SLOTS, 3, CX, NZ), f32), vm((SLOTS, 3, CX, NZ), f32),
        vm((SLOTS, 3, 1, NZ), f32), vm((SLOTS, 3, 1, NZ), f32),
        vm((SLOTS, 5, 1, NZ), f32), vm((SLOTS, GY, 1, LANES), f32),
        vm((3, NY, NZ), f32), vm((2, NY, NZ), f32), vm((3, CX, NZ), f32), vm((2, CX, NZ), f32),
        pltpu.SemaphoreType.DMA((10,)), pltpu.SemaphoreType.DMA((11,)),
        pltpu.SemaphoreType.DMA((11, SLOTS)), pltpu.SemaphoreType.DMA((4,)),
        pltpu.SemaphoreType.DMA((4,)),
    ]
    anywhere = pl.BlockSpec(memory_space=pltpu.HBM)
    return pl.pallas_call(
        kernel,
        out_shape=(
            jax.ShapeDtypeStruct((3, *block), f32),
            jax.ShapeDtypeStruct((6, *block), f32),
            jax.ShapeDtypeStruct((1, NY, NZ), f32),
        ),
        in_specs=[anywhere] * 10,
        out_specs=(pl.BlockSpec(memory_space=pltpu.VMEM),) * 3,
        scratch_shapes=scratch,
        compiler_params=pltpu.CompilerParams(
            collective_id=0, has_side_effects=True, vmem_limit_bytes=62 << 20
        ),
        name="fault_steps",
    )(*args)


def solution(mesh):
    wave = P(None, "gx", "gy", None)
    fault = P("gx", "gy", None)
    row = P("gx", None)
    return jax.shard_map(
        on_device,
        mesh=mesh,
        in_specs=(wave, wave, wave, wave, fault, fault, row, row, row, P("gx", None, None)),
        out_specs=(wave, wave, fault),
        check_vma=False,
    )
```

```python
import jax
import jax.numpy as jnp
from jax import lax
from jax.experimental import pallas as pl
from jax.experimental.pallas import tpu as pltpu
from jax.sharding import PartitionSpec as P

STEPS = 16
DT = 0.1
GX, GY, NX4 = 8, 16, 4
CX, NY, NZ = 8, 16, 256
LANES = 128
BLOCKS = NY * NZ // LANES
TOTAL = BLOCKS * GY
SEGS, MAXB = 32, 63
MESH = pl.DeviceIdType.MESH

YLO, YHI, C1, C2, XHI, XLO, LLO, LHI, C0, C3, SUMS = range(11)
EARLY, LATE = (YLO, YHI, C1, C2), (XHI, XLO, LLO, LHI, C0, C3)
LINES = (
    (3, 0), (5, 0), (1, 0), (0, 15), (3, 15), (4, 15), (5, 15), (2, 15), (1, 15), (0, 0), (2, 0)
)
VLINES = ((0, 15), (2, 15), (1, 0))
SLOTS = 4


def nodes(face):
    return jnp.concatenate([face[:, :LANES], face[:, LANES:]], axis=0)


def face_of(rows):
    return jnp.concatenate([rows[:NY], rows[NY:]], axis=1)


def lane_ids(rows):
    return lax.broadcasted_iota(jnp.int32, (rows, LANES), 1)


def up_z(f):
    lane = lane_ids(f.shape[0])
    a, b = f[:, :LANES], f[:, LANES:]
    ra, rb = pltpu.roll(a, LANES - 1, 1), pltpu.roll(b, LANES - 1, 1)
    last = lane == LANES - 1
    return jnp.concatenate([jnp.where(last, rb, ra), jnp.where(last, 0.0, rb)], axis=1)


def dn_z(f):
    lane = lane_ids(f.shape[0])
    a, b = f[:, :LANES], f[:, LANES:]
    ra, rb = pltpu.roll(a, 1, 1), pltpu.roll(b, 1, 1)
    first = lane == 0
    return jnp.concatenate([jnp.where(first, 0.0, ra), jnp.where(first, ra, rb)], axis=1)


def row_ids():
    return lax.broadcasted_iota(jnp.int32, (8, NZ), 0)


def up_y(f, halo):
    last = row_ids() == 7
    r0, r1 = pltpu.roll(f[:8], 7, 0), pltpu.roll(f[8:], 7, 0)
    return jnp.concatenate([jnp.where(last, r1, r0), jnp.where(last, halo, r1)], axis=0)


def dn_y(f, halo):
    first = row_ids() == 0
    r0, r1 = pltpu.roll(f[:8], 1, 0), pltpu.roll(f[8:], 1, 0)
    return jnp.concatenate([jnp.where(first, halo, r0), jnp.where(first, r0, r1)], axis=0)


def up_i(f):
    return jnp.where(row_ids() == 7, 0.0, pltpu.roll(f, 7, 0))


def dn_i(f):
    return jnp.where(row_ids() == 0, 0.0, pltpu.roll(f, 1, 0))


def hops(d):
    return min(d, NX4 - d)


def kernel(
    vel_h, str_h, mat_h, bg_h, load_h, slip_h, stat_h, dyn_h, weak_h, seg_h,
    v, s, slip_o,
    m, bg, load, slip, stat, dyn, weak, seg,
    same, coef, face, sn, g, gv, fm,
    xs_lo, xs_hi, ys_lo, ys_hi, ls_lo, ls_hi, cs,
    co, ixs_lo, ixs_hi, iys_lo, iys_hi, ics,
    xr_lo, xr_hi, yr_lo, yr_hi, lr_lo, lr_hi, cr, ar,
    hx_lo, hx_hi, hy_lo, hy_hi, kc,
    load_sem, send_sem, recv_sem, isend_sem, irecv_sem,
):
    gx, gy = lax.axis_index("gx"), lax.axis_index("gy")
    xm, xp = lax.rem(gx + GX - 1, GX), lax.rem(gx + 1, GX)
    ym, yp = lax.rem(gy + GY - 1, GY), lax.rem(gy + 1, GY)
    chip_y, chip_x = gy // NX4, lax.rem(gy, NX4)
    offsets = [(a, b) for a in range(NX4) for b in range(NX4) if a or b]
    offsets.sort(key=lambda o: -(hops(o[0]) + hops(o[1])))
    peers = [
        lax.rem(chip_y + a, NX4) * NX4 + lax.rem(chip_x + b, NX4) for a, b in offsets
    ]

    barrier = pltpu.get_barrier_semaphore()
    others = [(xm, gy), (xp, gy), (xm, ym), (xp, yp), (xp, ym), (xm, yp)]
    greet = [(gx, peer) for peer in peers] + others
    for dev in greet:
        pl.semaphore_signal(barrier, inc=1, device_id=dev, device_id_type=MESH)

    loads = [
        (seg_h.at[0], seg), (stat_h, stat), (dyn_h, dyn), (weak_h, weak),
        (slip_h.at[0], slip), (load_h.at[0], load), (bg_h.at[:, 0], bg),
        (mat_h, m), (str_h, s), (vel_h, v),
    ]
    copies = [
        pltpu.make_async_copy(src, dst, load_sem.at[i]) for i, (src, dst) in enumerate(loads)
    ]
    for copy in copies:
        copy.start()

    copies[0].wait()
    table = seg[...]

    def block_of(lane):
        c = lax.rem(lane, BLOCKS)
        return lane - c + 2 * lax.rem(c, NY) + c // NY

    lane_all = block_of(lax.broadcasted_iota(jnp.int32, (SEGS, TOTAL), 1))
    c = lane_ids(SEGS)
    own_block = jnp.where(c < BLOCKS, gy * BLOCKS + block_of(c), -1)
    member = jnp.zeros((SEGS, TOTAL), jnp.float32)
    own = jnp.zeros((SEGS, LANES), jnp.float32)
    for entry in range(MAXB):
        ids = table[:, entry : entry + 1]
        member = jnp.where(ids == lane_all, 1.0, member)
        own = jnp.where(ids == own_block, 1.0, own)
    own_t = own.T[:BLOCKS]
    shared = jnp.dot(own_t, member, preferred_element_type=jnp.float32)
    same[...] = shared
    count = jnp.sum(shared, axis=1, keepdims=True)
    for copy in copies[1:]:
        copy.wait()
    stat_b = jnp.sum(own_t * stat[...], axis=1, keepdims=True)
    dyn_b = jnp.sum(own_t * dyn[...], axis=1, keepdims=True)
    weak_b = jnp.sum(own_t * weak[...], axis=1, keepdims=True)
    wide = (BLOCKS, LANES)
    coef[0] = jnp.broadcast_to(-1.0 / (LANES * count * weak_b), wide)
    coef[1] = jnp.broadcast_to(stat_b - dyn_b, wide)
    coef[2] = jnp.broadcast_to(dyn_b, wide)

    face[0] = nodes(bg[0])
    face[1] = nodes(bg[1])
    face[2] = nodes(load[...])
    face[3] = 1.0 / nodes(m[1, 0])
    sn[...] = nodes(slip[...])
    for i in range(CX):
        for k in range(3):
            m[k, i] = m[k, i] * DT
        for k, (field, row) in enumerate(LINES):
            g[0, k, i : i + 1] = s[field, i, row : row + 1]
        for k in range(3):
            fm[k, 0, i : i + 1] = m[k, i, 0:1]
            fm[k, 1, i : i + 1] = m[k, i, 15:16]

    ixs_lo[0], ixs_lo[1] = m[2, 0], v[0, 0]
    ixs_hi[0], ixs_hi[1], ixs_hi[2] = m[2, 7], v[1, 7], v[2, 7]
    for i in range(CX):
        iys_lo[0, i : i + 1], iys_lo[1, i : i + 1] = m[2, i, 0:1], v[1, i, 0:1]
        iys_hi[0, i : i + 1], iys_hi[1, i : i + 1] = m[2, i, 15:16], v[0, i, 15:16]
        iys_hi[2, i : i + 1] = v[2, i, 15:16]
    ics[0], ics[1], ics[2] = m[0, 7, 15:16], m[1, 7, 15:16], m[1, 7, 0:1]
    co[...] = jnp.zeros_like(co)

    def remote(src, dst, send, recv, dev):
        return pltpu.make_async_remote_copy(
            src_ref=src, dst_ref=dst, send_sem=send, recv_sem=recv,
            device_id=dev, device_id_type=MESH,
        )

    def once_copies():
        return [
            remote(ixs_lo, hx_hi, isend_sem.at[0], irecv_sem.at[0], (xm, gy)),
            remote(ixs_hi, hx_lo, isend_sem.at[1], irecv_sem.at[1], (xp, gy)),
            remote(iys_lo, hy_hi, isend_sem.at[2], irecv_sem.at[2], (gx, ym)),
            remote(iys_hi, hy_lo, isend_sem.at[3], irecv_sem.at[3], (gx, yp)),
            remote(
                ics.at[pl.ds(0, 2)], kc.at[pl.ds(0, 2)], isend_sem.at[4], irecv_sem.at[4], (xp, yp)
            ),
            remote(
                ics.at[pl.ds(2, 1)], kc.at[pl.ds(2, 1)], isend_sem.at[5], irecv_sem.at[5], (xp, ym)
            ),
        ]

    def halo(kind, slot):
        def corner(first, size):
            return cs.at[pl.ds(first, size)], cr.at[slot, pl.ds(first, size)]

        src, dst, dev = {
            XHI: lambda: (xs_hi, xr_lo.at[slot], (xp, gy)),
            YLO: lambda: (ys_lo, yr_hi.at[slot], (gx, ym)),
            YHI: lambda: (ys_hi, yr_lo.at[slot], (gx, yp)),
            C1: lambda: (*corner(1, 2), (xp, yp)),
            C2: lambda: (*corner(3, 1), (xp, ym)),
            XLO: lambda: (xs_lo, xr_hi.at[slot], (xm, gy)),
            LLO: lambda: (ls_lo, lr_hi.at[slot], (gx, ym)),
            LHI: lambda: (ls_hi, lr_lo.at[slot], (gx, yp)),
            C0: lambda: (*corner(0, 1), (xm, ym)),
            C3: lambda: (*corner(4, 1), (xm, yp)),
        }[kind]()
        return remote(src, dst, send_sem.at[kind], recv_sem.at[kind, slot], dev)

    def sums_wait(slot, sem):
        part = ar.at[slot, pl.ds(0, GY - 1)]
        pltpu.make_async_copy(part, part, sem).wait()

    block_lane = lax.rem(gy, 4) * BLOCKS + lax.broadcasted_iota(jnp.int32, wide, 0)
    place = block_lane == lane_ids(BLOCKS)

    def send_sums(slot, slip_now):
        sums = jnp.sum(slip_now, axis=1, keepdims=True)
        row = jnp.sum(jnp.where(place, sums, 0.0), axis=0, keepdims=True)
        ar[slot, gy] = row
        for peer in peers:
            remote(
                ar.at[slot, gy], ar.at[slot, gy],
                send_sem.at[SUMS], recv_sem.at[SUMS, slot], (gx, peer),
            ).start()

    def lines(edge):
        g0, g1, g4, g5, g7 = (g[edge, k] for k in (0, 1, 4, 5, 7))
        to_lo = up_i(g0) - g0 + g[edge, 2] + (up_z(g1) - g1)
        to_hi_x = g[edge, 3] - dn_i(g[edge, 3]) - g4 + (up_z(g5) - g5)
        to_hi_z = up_i(g5) - g5 - g[edge, 6] + (g7 - dn_z(g7))
        return to_lo, to_hi_x, to_hi_z

    def send_corners(slot):
        cs[1] = g[slot, 3, 7:8]
        cs[2] = g[slot, 8, 7:8]
        cs[3] = g[slot, 1, 7:8]
        halo(C1, slot).start()
        halo(C2, slot).start()

    def send_lines(slot):
        to_lo, to_hi_x, to_hi_z = lines(slot)
        ys_lo[0], ys_lo[1], ys_lo[2] = g[slot, 0], g[slot, 1], to_lo
        halo(YLO, slot).start()
        ys_hi[0], ys_hi[1], ys_hi[2] = g[slot, 8], to_hi_x, to_hi_z
        halo(YHI, slot).start()

    def send_late(slot, xy, xz, slip_now):
        cs[0] = xy[0:1]
        cs[4] = xz[15:]
        halo(C0, slot).start()
        halo(C3, slot).start()
        to_lo, to_hi_x, to_hi_z = lines(slot)
        ls_lo[0], ls_lo[1], ls_lo[2] = g[slot, 0, 0:1], g[slot, 1, 0:1], to_lo[0:1]
        halo(LLO, slot).start()
        ls_hi[0], ls_hi[1], ls_hi[2] = g[slot, 8, 0:1], to_hi_x[0:1], to_hi_z[0:1]
        halo(LHI, slot).start()
        send_sums(slot, slip_now)

    def send_rows(slot):
        xy, xz = s[3, 0], s[4, 0]
        xs_lo[0] = xy
        xs_lo[1] = xz
        xs_lo[2] = s[0, 0] + (up_y(xy, 0.0) - xy) + (up_z(xz) - xz)
        halo(XLO, slot).start()
        yy, zz, yz = s[1, 7], s[2, 7], s[5, 7]
        xs_hi[0] = s[0, 7]
        xs_hi[1] = (yy - dn_y(yy, 0.0)) - s[3, 7] + (up_z(yz) - yz)
        xs_hi[2] = (up_y(yz, 0.0) - yz) - s[4, 7] + (zz - dn_z(zz))
        halo(XHI, slot).start()

    pl.semaphore_wait(barrier, len(greet))
    for copy in once_copies():
        copy.start()
    send_corners(0)
    send_lines(0)
    send_late(0, s[3, 0], s[4, 0], sn[...])
    send_rows(0)
    for copy in once_copies():
        copy.wait_recv()

    def advance(t, carry):
        now, later = lax.rem(t, SLOTS), lax.rem(t + 1, SLOTS)

        for kind in (XLO, XHI):
            halo(kind, now).wait_recv()
        vx_xp = hx_hi[1] + hx_hi[0] * (xr_hi[now, 2] - s[0, 7])
        vy_xm = hx_lo[1] + hx_lo[0] * (xr_lo[now, 1] + s[3, 0])
        vz_xm = hx_lo[2] + hx_lo[0] * (xr_lo[now, 2] + s[4, 0])
        hx_hi[1], hx_lo[1], hx_lo[2] = vx_xp, vy_xm, vz_xm
        for i in range(CX):
            b = m[2, i]
            row = slice(i, i + 1)
            xx_m = s[0, i - 1] if i else xr_lo[now, 0]
            xy_p = s[3, i + 1] if i < CX - 1 else xr_hi[now, 0]
            xz_p = s[4, i + 1] if i < CX - 1 else xr_hi[now, 1]
            xx, yy, zz, xy, xz, yz = (s[k, i] for k in range(6))
            vx = v[0, i] + b * ((xx - xx_m) + (up_y(xy, 0.0) - xy) + (up_z(xz) - xz))
            vy = v[1, i] + b * ((xy_p - xy) + (yy - dn_y(yy, 0.0)) + (up_z(yz) - yz))
            vz = v[2, i] + b * ((xz_p - xz) + (up_y(yz, 0.0) - yz) + (zz - dn_z(zz)))
            v[0, i], v[1, i], v[2, i] = vx, vy, vz
            gv[0, row], gv[1, row], gv[2, row] = vx[15:], vz[15:], vy[0:1]
        for i in range(CX):
            lam, mu = m[0, i], m[1, i]
            row = slice(i, i + 1)
            vx, vy, vz = v[0, i], v[1, i], v[2, i]
            vx_p = v[0, i + 1] if i < CX - 1 else vx_xp
            vy_m = v[1, i - 1] if i else vy_xm
            vz_m = v[2, i - 1] if i else vz_xm
            ex = vx_p - vx
            ey = up_y(vy, 0.0) - vy
            ez = up_z(vz) - vz
            bulk = lam * (ex + ey + ez)
            mu2 = mu + mu
            fields = (
                s[0, i] + (bulk + mu2 * ex),
                s[1, i] + (bulk + mu2 * ey),
                s[2, i] + (bulk + mu2 * ez),
                s[3, i] + mu * ((vy - vy_m) + (vx - dn_y(vx, 0.0))),
                s[4, i] + mu * ((vz - vz_m) + (vx - dn_z(vx))),
                s[5, i] + mu * ((vz - dn_y(vz, 0.0)) + (vy - dn_z(vy))),
            )
            if i == 0:
                xy_row, xz_row = fields[3], fields[4]
            for k, field in enumerate(fields):
                s[k, i] = field
            for k, (field, line) in enumerate(LINES):
                g[later, k, row] = fields[field][line : line + 1]

        for kind in (YLO, YHI, LLO, LHI, C1, C2):
            halo(kind, now).wait_recv()
        first, last = row_ids() == 0, row_ids() == 7
        up_xy, up_yz, acc_vy = (
            jnp.where(first, lr_hi[now, k], yr_hi[now, k]) for k in range(3)
        )
        dn_yy, acc_vx, acc_vz = (
            jnp.where(first, lr_lo[now, k], yr_lo[now, k]) for k in range(3)
        )
        dex, dey = hy_lo[0, 0:1] * co[0], hx_lo[0, 0:1] * co[0]
        bulk = kc[0] * (dex + dey)
        corner1 = cr[now, 1] + (bulk + (kc[1] + kc[1]) * dex)
        corner2 = cr[now, 2] + (bulk + (kc[1] + kc[1]) * dey)
        corner3 = cr[now, 3] - kc[2] * (hx_lo[0, 15:16] * co[1])
        vx_ym = hy_lo[1] + hy_lo[0] * (acc_vx + g[now, 0] - jnp.where(first, corner1, 0.0))
        vz_ym = hy_lo[2] + hy_lo[0] * (acc_vz + g[now, 1])
        vy_yp = hy_hi[1] + hy_hi[0] * (acc_vy - g[now, 8])
        hy_lo[1], hy_lo[2], hy_hi[1] = vx_ym, vz_ym, vy_yp
        dvy_xm = -hx_lo[0, 0:1] * corner2
        dvz_xm = hx_lo[0, 15:16] * corner3
        hx_lo[1, 0:1] = hx_lo[1, 0:1] + dvy_xm
        hx_lo[2, 15:16] = hx_lo[2, 15:16] + dvz_xm
        dvx, dvz, dvy = fm[2, 1] * up_xy, fm[2, 1] * up_yz, -fm[2, 0] * dn_yy
        gv[0], gv[1], gv[2] = gv[0] + dvx, gv[1] + dvz, gv[2] + dvy
        lam, mu = fm[0, 1], fm[1, 1]
        ex = up_i(dvx) - dvx
        ez = up_z(dvz) - dvz
        bulk = lam * (ex + vy_yp + ez)
        mu2 = mu + mu
        dvz_m = jnp.where(first, dvz_xm, pltpu.roll(dvz, 1, 0))
        xy15 = g[later, 4] + mu * dvx
        xz15 = g[later, 5] + mu * ((dvz - dvz_m) + (dvx - dn_z(dvx)))
        g[later, 3] = g[later, 3] + (bulk + mu2 * ex)
        g[later, 8] = g[later, 8] + (bulk + mu2 * vy_yp)
        g[later, 7] = g[later, 7] + (bulk + mu2 * ez)
        g[later, 4] = xy15
        g[later, 5] = xz15
        g[later, 6] = g[later, 6] + mu * dvz
        lam, mu = fm[0, 0], fm[1, 0]
        bulk = lam * dvy
        dvy_m = jnp.where(first, dvy_xm, pltpu.roll(dvy, 1, 0))
        xy00 = g[later, 0] + mu * ((dvy - dvy_m) - vx_ym)
        g[later, 9] = g[later, 9] - bulk
        g[later, 10] = g[later, 10] - bulk
        g[later, 2] = g[later, 2] - (bulk + (mu + mu) * dvy)
        g[later, 0] = xy00
        g[later, 1] = g[later, 1] + mu * ((dvy - dn_z(dvy)) - vz_ym)

        @pl.when(t < STEPS - 1)
        def _():
            for kind in (C1, C2):
                halo(kind, now).wait_send()
            send_corners(later)

        for kind in (C0, C3):
            halo(kind, now).wait_recv()
        corner0, corner4 = cr[now, 0], cr[now, 4]
        dvx_xp = hx_hi[0, 15:16] * corner0
        hx_hi[1, 15:16] = hx_hi[1, 15:16] + dvx_xp
        dvy_yp = hy_hi[0, 7:8] * corner0
        hy_hi[1, 7:8] = hy_hi[1, 7:8] + dvy_yp
        dvz_ym = hy_lo[0, 7:8] * corner4
        hy_lo[2, 7:8] = hy_lo[2, 7:8] + dvz_ym
        lam, mu2 = fm[0, 1, 7:8], fm[1, 1, 7:8] + fm[1, 1, 7:8]
        bulk = lam * (dvx_xp + dvy_yp)
        g[later, 3, 7:8] = g[later, 3, 7:8] + (bulk + mu2 * dvx_xp)
        g[later, 8, 7:8] = g[later, 8, 7:8] + (bulk + mu2 * dvy_yp)
        g[later, 7, 7:8] = g[later, 7, 7:8] + bulk
        g[later, 1, 7:8] = g[later, 1, 7:8] - fm[1, 0, 7:8] * dvz_ym

        @pl.when(t < STEPS - 1)
        def _():
            for kind in (YLO, YHI):
                halo(kind, now).wait_send()
            send_lines(later)

        def patch(row, line0, line15):
            low = row[:8] if line0 is None else jnp.where(first, line0, row[:8])
            return jnp.concatenate([low, jnp.where(last, line15, row[8:])], axis=0)

        xy0 = patch(xy_row, xy00[0:1], xy15[0:1])
        xz0 = patch(xz_row, None, xz15[0:1])
        trial_y = nodes(xy0) + face[0]
        trial_z = nodes(xz0) + face[1]
        mag = jnp.sqrt(trial_y * trial_y + trial_z * trial_z)
        load_ratio = face[2] / mag
        rate = mag * face[3]

        sums_wait(now, recv_sem.at[SUMS, now])
        total = jnp.zeros(wide, jnp.float32)
        for q in range(4):
            part = ar[now, 4 * q] + ar[now, 4 * q + 1] + ar[now, 4 * q + 2] + ar[now, 4 * q + 3]
            total = total + same[:, q * LANES : (q + 1) * LANES] * part
        seg_sum = jnp.sum(total, axis=1, keepdims=True)
        friction = coef[2] + coef[1] * jnp.exp(seg_sum * coef[0])
        excess = 1.0 - jnp.minimum(friction * load_ratio, 1.0)
        slip_now = sn[...] + rate * excess
        sn[...] = slip_now
        xy = xy0 - face_of(trial_y * excess)
        xz = xz0 - face_of(trial_z * excess)
        s[3, 0] = xy
        s[4, 0] = xz
        g[later, 0, 0:1], g[later, 4, 0:1], g[later, 5, 0:1] = xy[0:1], xy[15:], xz[15:]

        @pl.when(t < STEPS - 1)
        def _():
            for kind in LATE:
                halo(kind, now).wait_send()
            sums_wait(now, send_sem.at[SUMS])
            co[0], co[1] = cs[0], cs[4]
            send_late(later, xy, xz, slip_now)

        for i in range(CX):
            row = slice(i, i + 1)
            for k, (field, line) in enumerate(LINES):
                s[field, i, line : line + 1] = g[later, k, row]
            for k, (field, line) in enumerate(VLINES):
                v[field, i, line : line + 1] = gv[k, row]

        @pl.when(t < STEPS - 1)
        def _():
            send_rows(later)

        return carry

    lax.fori_loop(0, STEPS, advance, 0)

    slip_o[0] = face_of(sn[...])
    for kind in EARLY + LATE:
        halo(kind, 0).wait_send()
    sums_wait(0, send_sem.at[SUMS])
    for copy in once_copies():
        copy.wait_send()


def hand_over(vel_i, str_i, slip_i, vel_o, str_o, slip_o, v, s, slip, in_sem, out_sem):
    pieces = [(vel_i.at[k], v.at[k], vel_o.at[k]) for k in range(3)]
    pieces += [(str_i.at[k], s.at[k], str_o.at[k]) for k in range(6)]
    pieces.append((slip_i, slip, slip_o))
    ins = [pltpu.make_async_copy(a, b, in_sem.at[k]) for k, (a, b, _) in enumerate(pieces)]
    outs = [pltpu.make_async_copy(b, c, out_sem.at[k]) for k, (_, b, c) in enumerate(pieces)]
    for copy in ins:
        copy.start()
    for copy, out in zip(ins, outs):
        copy.wait()
        out.start()
    for out in outs:
        out.wait()


def on_device(*args):
    f32 = jnp.float32
    vm = pltpu.VMEM
    block = (CX, NY, NZ)
    scratch = [
        vm((3, *block), f32),
        vm((2, NY, NZ), f32), vm((NY, NZ), f32), vm((NY, NZ), f32),
        vm((1, SEGS), f32), vm((1, SEGS), f32), vm((1, SEGS), f32),
        vm((SEGS, MAXB), jnp.int32),
        vm((BLOCKS, TOTAL), f32), vm((3, BLOCKS, LANES), f32), vm((4, BLOCKS, LANES), f32),
        vm((BLOCKS, LANES), f32), vm((SLOTS, len(LINES), CX, NZ), f32),
        vm((3, CX, NZ), f32), vm((3, 2, CX, NZ), f32),
        vm((3, NY, NZ), f32), vm((3, NY, NZ), f32), vm((3, CX, NZ), f32), vm((3, CX, NZ), f32),
        vm((3, 1, NZ), f32), vm((3, 1, NZ), f32), vm((5, 1, NZ), f32),
        vm((2, 1, NZ), f32),
        vm((2, NY, NZ), f32), vm((3, NY, NZ), f32), vm((2, CX, NZ), f32), vm((3, CX, NZ), f32),
        vm((3, 1, NZ), f32),
        vm((SLOTS, 3, NY, NZ), f32), vm((SLOTS, 3, NY, NZ), f32),
        vm((SLOTS, 3, CX, NZ), f32), vm((SLOTS, 3, CX, NZ), f32),
        vm((SLOTS, 3, 1, NZ), f32), vm((SLOTS, 3, 1, NZ), f32),
        vm((SLOTS, 5, 1, NZ), f32), vm((SLOTS, GY, 1, LANES), f32),
        vm((3, NY, NZ), f32), vm((2, NY, NZ), f32), vm((3, CX, NZ), f32), vm((2, CX, NZ), f32),
        vm((3, 1, NZ), f32),
        pltpu.SemaphoreType.DMA((10,)), pltpu.SemaphoreType.DMA((11,)),
        pltpu.SemaphoreType.DMA((11, SLOTS)), pltpu.SemaphoreType.DMA((6,)),
        pltpu.SemaphoreType.DMA((6,)),
    ]
    anywhere = pl.BlockSpec(memory_space=pltpu.HBM)
    shapes = (
        jax.ShapeDtypeStruct((3, *block), f32),
        jax.ShapeDtypeStruct((6, *block), f32),
        jax.ShapeDtypeStruct((1, NY, NZ), f32),
    )
    results = pl.pallas_call(
        kernel,
        out_shape=shapes,
        in_specs=[anywhere] * 10,
        out_specs=(pl.BlockSpec(memory_space=pltpu.VMEM),) * 3,
        scratch_shapes=scratch,
        compiler_params=pltpu.CompilerParams(
            collective_id=0, has_side_effects=True, vmem_limit_bytes=62 << 20
        ),
        name="fault_steps",
    )(*args)
    return pl.pallas_call(
        hand_over,
        out_shape=shapes,
        in_specs=[anywhere] * 3,
        out_specs=(anywhere,) * 3,
        scratch_shapes=[
            vm((3, *block), f32), vm((6, *block), f32), vm((1, NY, NZ), f32),
            pltpu.SemaphoreType.DMA((10,)), pltpu.SemaphoreType.DMA((10,)),
        ],
        compiler_params=pltpu.CompilerParams(vmem_limit_bytes=62 << 20),
        name="hand_over",
    )(*results)


def solution(mesh):
    wave = P(None, "gx", "gy", None)
    fault = P("gx", "gy", None)
    row = P("gx", None)
    return jax.shard_map(
        on_device,
        mesh=mesh,
        in_specs=(wave, wave, wave, wave, fault, fault, row, row, row, P("gx", None, None)),
        out_specs=(wave, wave, fault),
        check_vma=False,
    )
```

```python
import jax
import jax.numpy as jnp
from jax import lax
from jax.experimental import pallas as pl
from jax.experimental.pallas import tpu as pltpu
from jax.sharding import PartitionSpec as P

STEPS = 16
DT = 0.1
GX, GY, NX4 = 8, 16, 4
CX, NY, NZ = 8, 16, 256
LANES = 128
BLOCKS = NY * NZ // LANES
TOTAL = BLOCKS * GY
SEGS, MAXB = 32, 63
MESH = pl.DeviceIdType.MESH

YLO, YHI, C1, C2, XHI, XLO, LLO, LHI, C0, C3, SUMS = range(11)
EARLY, LATE = (YLO, YHI, C1, C2), (XHI, XLO, LLO, LHI, C0, C3)
LINES = (
    (3, 0), (5, 0), (1, 0), (0, 15), (3, 15), (4, 15), (5, 15), (2, 15), (1, 15), (0, 0), (2, 0)
)
VLINES = ((0, 15), (2, 15), (1, 0))
SLOTS = 4
FAR = 5


def nodes(face):
    return jnp.concatenate([face[:, :LANES], face[:, LANES:]], axis=0)


def face_of(rows):
    return jnp.concatenate([rows[:NY], rows[NY:]], axis=1)


def lane_ids(rows):
    return lax.broadcasted_iota(jnp.int32, (rows, LANES), 1)


def up_z(f):
    lane = lane_ids(f.shape[0])
    a, b = f[:, :LANES], f[:, LANES:]
    ra, rb = pltpu.roll(a, LANES - 1, 1), pltpu.roll(b, LANES - 1, 1)
    last = lane == LANES - 1
    return jnp.concatenate([jnp.where(last, rb, ra), jnp.where(last, 0.0, rb)], axis=1)


def dn_z(f):
    lane = lane_ids(f.shape[0])
    a, b = f[:, :LANES], f[:, LANES:]
    ra, rb = pltpu.roll(a, 1, 1), pltpu.roll(b, 1, 1)
    first = lane == 0
    return jnp.concatenate([jnp.where(first, 0.0, ra), jnp.where(first, ra, rb)], axis=1)


def row_ids():
    return lax.broadcasted_iota(jnp.int32, (8, NZ), 0)


def up_y(f, halo):
    last = row_ids() == 7
    r0, r1 = pltpu.roll(f[:8], 7, 0), pltpu.roll(f[8:], 7, 0)
    return jnp.concatenate([jnp.where(last, r1, r0), jnp.where(last, halo, r1)], axis=0)


def dn_y(f, halo):
    first = row_ids() == 0
    r0, r1 = pltpu.roll(f[:8], 1, 0), pltpu.roll(f[8:], 1, 0)
    return jnp.concatenate([jnp.where(first, halo, r0), jnp.where(first, r0, r1)], axis=0)


def up_i(f):
    return jnp.where(row_ids() == 7, 0.0, pltpu.roll(f, 7, 0))


def dn_i(f):
    return jnp.where(row_ids() == 0, 0.0, pltpu.roll(f, 1, 0))


def hops(d):
    return min(d, NX4 - d)


def kernel(
    vel_h, str_h, mat_h, bg_h, load_h, slip_h, stat_h, dyn_h, weak_h, seg_h,
    vel_o, str_o, slip_o,
    v, s, m, bg, load, slip, stat, dyn, weak, seg,
    same, coef, face, sn, g, gv, fm,
    xs_lo, xs_hi, ys_lo, ys_hi, ls_lo, ls_hi, cs,
    co, ixs_lo, ixs_hi, iys_lo, iys_hi, ics,
    xr_lo, xr_hi, yr_lo, yr_hi, lr_lo, lr_hi, cr, ar,
    hx_lo, hx_hi, hy_lo, hy_hi, kc,
    load_sem, send_sem, recv_sem, isend_sem, irecv_sem, out_sem,
):
    gx, gy = lax.axis_index("gx"), lax.axis_index("gy")
    xm, xp = lax.rem(gx + GX - 1, GX), lax.rem(gx + 1, GX)
    ym, yp = lax.rem(gy + GY - 1, GY), lax.rem(gy + 1, GY)
    chip_y, chip_x = gy // NX4, lax.rem(gy, NX4)
    offsets = [(a, b) for a in range(NX4) for b in range(NX4) if a or b]
    offsets.sort(key=lambda o: -(hops(o[0]) + hops(o[1])))
    peers = [
        lax.rem(chip_y + a, NX4) * NX4 + lax.rem(chip_x + b, NX4) for a, b in offsets
    ]

    barrier = pltpu.get_barrier_semaphore()
    others = [(xm, gy), (xp, gy), (xm, ym), (xp, yp), (xp, ym), (xm, yp)]
    greet = [(gx, peer) for peer in peers] + others
    for dev in greet:
        pl.semaphore_signal(barrier, inc=1, device_id=dev, device_id_type=MESH)

    loads = [
        (seg_h.at[0], seg), (stat_h, stat), (dyn_h, dyn), (weak_h, weak),
        (slip_h.at[0], slip), (load_h.at[0], load), (bg_h.at[:, 0], bg),
        (mat_h, m), (str_h, s), (vel_h, v),
    ]
    copies = [
        pltpu.make_async_copy(src, dst, load_sem.at[i]) for i, (src, dst) in enumerate(loads)
    ]
    for copy in copies:
        copy.start()

    copies[0].wait()
    table = seg[...]

    def block_of(lane):
        c = lax.rem(lane, BLOCKS)
        return lane - c + 2 * lax.rem(c, NY) + c // NY

    lane_all = block_of(lax.broadcasted_iota(jnp.int32, (SEGS, TOTAL), 1))
    c = lane_ids(SEGS)
    own_block = jnp.where(c < BLOCKS, gy * BLOCKS + block_of(c), -1)
    member = jnp.zeros((SEGS, TOTAL), jnp.float32)
    own = jnp.zeros((SEGS, LANES), jnp.float32)
    for entry in range(MAXB):
        ids = table[:, entry : entry + 1]
        member = jnp.where(ids == lane_all, 1.0, member)
        own = jnp.where(ids == own_block, 1.0, own)
    own_t = own.T[:BLOCKS]
    shared = jnp.dot(own_t, member, preferred_element_type=jnp.float32)
    same[...] = shared
    count = jnp.sum(shared, axis=1, keepdims=True)
    for copy in copies[1:]:
        copy.wait()
    stat_b = jnp.sum(own_t * stat[...], axis=1, keepdims=True)
    dyn_b = jnp.sum(own_t * dyn[...], axis=1, keepdims=True)
    weak_b = jnp.sum(own_t * weak[...], axis=1, keepdims=True)
    wide = (BLOCKS, LANES)
    coef[0] = jnp.broadcast_to(-1.0 / (LANES * count * weak_b), wide)
    coef[1] = jnp.broadcast_to(stat_b - dyn_b, wide)
    coef[2] = jnp.broadcast_to(dyn_b, wide)

    face[0] = nodes(bg[0])
    face[1] = nodes(bg[1])
    face[2] = nodes(load[...])
    face[3] = 1.0 / nodes(m[1, 0])
    sn[...] = nodes(slip[...])
    for i in range(CX):
        for k in range(3):
            m[k, i] = m[k, i] * DT
        for k, (field, row) in enumerate(LINES):
            g[0, k, i : i + 1] = s[field, i, row : row + 1]
        for k in range(3):
            fm[k, 0, i : i + 1] = m[k, i, 0:1]
            fm[k, 1, i : i + 1] = m[k, i, 15:16]

    ixs_lo[0], ixs_lo[1] = m[2, 0], v[0, 0]
    ixs_hi[0], ixs_hi[1], ixs_hi[2] = m[2, 7], v[1, 7], v[2, 7]
    for i in range(CX):
        iys_lo[0, i : i + 1], iys_lo[1, i : i + 1] = m[2, i, 0:1], v[1, i, 0:1]
        iys_hi[0, i : i + 1], iys_hi[1, i : i + 1] = m[2, i, 15:16], v[0, i, 15:16]
        iys_hi[2, i : i + 1] = v[2, i, 15:16]
    ics[0], ics[1], ics[2] = m[0, 7, 15:16], m[1, 7, 15:16], m[1, 7, 0:1]
    co[...] = jnp.zeros_like(co)

    def remote(src, dst, send, recv, dev):
        return pltpu.make_async_remote_copy(
            src_ref=src, dst_ref=dst, send_sem=send, recv_sem=recv,
            device_id=dev, device_id_type=MESH,
        )

    def once_copies():
        return [
            remote(ixs_lo, hx_hi, isend_sem.at[0], irecv_sem.at[0], (xm, gy)),
            remote(ixs_hi, hx_lo, isend_sem.at[1], irecv_sem.at[1], (xp, gy)),
            remote(iys_lo, hy_hi, isend_sem.at[2], irecv_sem.at[2], (gx, ym)),
            remote(iys_hi, hy_lo, isend_sem.at[3], irecv_sem.at[3], (gx, yp)),
            remote(
                ics.at[pl.ds(0, 2)], kc.at[pl.ds(0, 2)], isend_sem.at[4], irecv_sem.at[4], (xp, yp)
            ),
            remote(
                ics.at[pl.ds(2, 1)], kc.at[pl.ds(2, 1)], isend_sem.at[5], irecv_sem.at[5], (xp, ym)
            ),
        ]

    def halo(kind, slot):
        def corner(first, size):
            return cs.at[pl.ds(first, size)], cr.at[slot, pl.ds(first, size)]

        src, dst, dev = {
            XHI: lambda: (xs_hi, xr_lo.at[slot], (xp, gy)),
            YLO: lambda: (ys_lo, yr_hi.at[slot], (gx, ym)),
            YHI: lambda: (ys_hi, yr_lo.at[slot], (gx, yp)),
            C1: lambda: (*corner(1, 2), (xp, yp)),
            C2: lambda: (*corner(3, 1), (xp, ym)),
            XLO: lambda: (xs_lo, xr_hi.at[slot], (xm, gy)),
            LLO: lambda: (ls_lo, lr_hi.at[slot], (gx, ym)),
            LHI: lambda: (ls_hi, lr_lo.at[slot], (gx, yp)),
            C0: lambda: (*corner(0, 1), (xm, ym)),
            C3: lambda: (*corner(4, 1), (xm, yp)),
        }[kind]()
        return remote(src, dst, send_sem.at[kind], recv_sem.at[kind, slot], dev)

    def sums_wait(slot, sem):
        part = ar.at[slot, pl.ds(0, GY - 1)]
        pltpu.make_async_copy(part, part, sem).wait()

    block_lane = lax.rem(gy, 4) * BLOCKS + lax.broadcasted_iota(jnp.int32, wide, 0)
    place = block_lane == lane_ids(BLOCKS)

    def stage_sums(slot, slip_now):
        sums = jnp.sum(slip_now, axis=1, keepdims=True)
        ar[slot, gy] = jnp.sum(jnp.where(place, sums, 0.0), axis=0, keepdims=True)

    def send_sums(slot, targets):
        for peer in targets:
            remote(
                ar.at[slot, gy], ar.at[slot, gy],
                send_sem.at[SUMS], recv_sem.at[SUMS, slot], (gx, peer),
            ).start()

    def lines(edge):
        g0, g1, g4, g5, g7 = (g[edge, k] for k in (0, 1, 4, 5, 7))
        to_lo = up_i(g0) - g0 + g[edge, 2] + (up_z(g1) - g1)
        to_hi_x = g[edge, 3] - dn_i(g[edge, 3]) - g4 + (up_z(g5) - g5)
        to_hi_z = up_i(g5) - g5 - g[edge, 6] + (g7 - dn_z(g7))
        return to_lo, to_hi_x, to_hi_z

    def send_corners(slot):
        cs[1] = g[slot, 3, 7:8]
        cs[2] = g[slot, 8, 7:8]
        cs[3] = g[slot, 1, 7:8]
        halo(C1, slot).start()
        halo(C2, slot).start()

    def send_lines(slot):
        to_lo, to_hi_x, to_hi_z = lines(slot)
        ys_lo[0], ys_lo[1], ys_lo[2] = g[slot, 0], g[slot, 1], to_lo
        halo(YLO, slot).start()
        ys_hi[0], ys_hi[1], ys_hi[2] = g[slot, 8], to_hi_x, to_hi_z
        halo(YHI, slot).start()

    def send_late(slot, xy, xz, dy, dz, slip_now):
        cs[0] = xy[0:1]
        cs[4] = xz[15:]
        halo(C0, slot).start()
        halo(C3, slot).start()
        if slip_now is not None:
            stage_sums(slot, slip_now)
            send_sums(slot, peers[:FAR])
        ls_lo[0], ls_lo[1], ls_lo[2] = xy[0:1], g[slot, 1, 0:1], ys_lo[2, 0:1] + dy[0:1]
        halo(LLO, slot).start()
        dz15 = dz[15:]
        ls_hi[0] = g[slot, 8, 0:1]
        ls_hi[1] = ys_hi[1, 0:1] + dy[15:] - (up_z(dz15) - dz15)
        ls_hi[2] = ys_hi[2, 0:1] + dz15
        halo(LHI, slot).start()
        if slip_now is not None:
            send_sums(slot, peers[FAR:])

    def send_rows(slot):
        xy, xz = s[3, 0], s[4, 0]
        xs_lo[0] = xy
        xs_lo[1] = xz
        xs_lo[2] = s[0, 0] + (up_y(xy, 0.0) - xy) + (up_z(xz) - xz)
        halo(XLO, slot).start()
        yy, zz, yz = s[1, 7], s[2, 7], s[5, 7]
        xs_hi[0] = s[0, 7]
        xs_hi[1] = (yy - dn_y(yy, 0.0)) - s[3, 7] + (up_z(yz) - yz)
        xs_hi[2] = (up_y(yz, 0.0) - yz) - s[4, 7] + (zz - dn_z(zz))
        halo(XHI, slot).start()

    stage_sums(0, sn[...])
    pl.semaphore_wait(barrier, len(greet))
    send_sums(0, peers)
    for copy in once_copies():
        copy.start()
    send_corners(0)
    send_lines(0)
    still = jnp.zeros((NY, NZ), jnp.float32)
    send_late(0, s[3, 0], s[4, 0], still, still, None)
    send_rows(0)
    for copy in once_copies():
        copy.wait_recv()

    def write_back(edge):
        for i in range(CX):
            row = slice(i, i + 1)
            for k, (field, line) in enumerate(LINES):
                s[field, i, line : line + 1] = g[edge, k, row]
            for k, (field, line) in enumerate(VLINES):
                v[field, i, line : line + 1] = gv[k, row]

    rest = pl.ds(1, CX - 1)
    outs = [
        (v, vel_o), (s.at[:, rest], str_o.at[:, rest]),
        (s.at[:, pl.ds(0, 1)], str_o.at[:, pl.ds(0, 1)]), (slip, slip_o.at[0]),
    ]

    def out_copy(k):
        return pltpu.make_async_copy(*outs[k], out_sem.at[k])

    def advance(t, carry):
        now, later = lax.rem(t, SLOTS), lax.rem(t + 1, SLOTS)

        for kind in (XLO, XHI):
            halo(kind, now).wait_recv()
        vx_xp = hx_hi[1] + hx_hi[0] * (xr_hi[now, 2] - s[0, 7])
        vy_xm = hx_lo[1] + hx_lo[0] * (xr_lo[now, 1] + s[3, 0])
        vz_xm = hx_lo[2] + hx_lo[0] * (xr_lo[now, 2] + s[4, 0])
        hx_hi[1], hx_lo[1], hx_lo[2] = vx_xp, vy_xm, vz_xm
        for i in range(CX):
            b = m[2, i]
            row = slice(i, i + 1)
            xx_m = s[0, i - 1] if i else xr_lo[now, 0]
            xy_p = s[3, i + 1] if i < CX - 1 else xr_hi[now, 0]
            xz_p = s[4, i + 1] if i < CX - 1 else xr_hi[now, 1]
            xx, yy, zz, xy, xz, yz = (s[k, i] for k in range(6))
            vx = v[0, i] + b * ((xx - xx_m) + (up_y(xy, 0.0) - xy) + (up_z(xz) - xz))
            vy = v[1, i] + b * ((xy_p - xy) + (yy - dn_y(yy, 0.0)) + (up_z(yz) - yz))
            vz = v[2, i] + b * ((xz_p - xz) + (up_y(yz, 0.0) - yz) + (zz - dn_z(zz)))
            v[0, i], v[1, i], v[2, i] = vx, vy, vz
            gv[0, row], gv[1, row], gv[2, row] = vx[15:], vz[15:], vy[0:1]
        for i in range(CX):
            lam, mu = m[0, i], m[1, i]
            row = slice(i, i + 1)
            vx, vy, vz = v[0, i], v[1, i], v[2, i]
            vx_p = v[0, i + 1] if i < CX - 1 else vx_xp
            vy_m = v[1, i - 1] if i else vy_xm
            vz_m = v[2, i - 1] if i else vz_xm
            ex = vx_p - vx
            ey = up_y(vy, 0.0) - vy
            ez = up_z(vz) - vz
            bulk = lam * (ex + ey + ez)
            mu2 = mu + mu
            fields = (
                s[0, i] + (bulk + mu2 * ex),
                s[1, i] + (bulk + mu2 * ey),
                s[2, i] + (bulk + mu2 * ez),
                s[3, i] + mu * ((vy - vy_m) + (vx - dn_y(vx, 0.0))),
                s[4, i] + mu * ((vz - vz_m) + (vx - dn_z(vx))),
                s[5, i] + mu * ((vz - dn_y(vz, 0.0)) + (vy - dn_z(vy))),
            )
            if i == 0:
                xy_row, xz_row = fields[3], fields[4]
            for k, field in enumerate(fields):
                s[k, i] = field
            for k, (field, line) in enumerate(LINES):
                g[later, k, row] = fields[field][line : line + 1]

        for kind in (YLO, YHI, LLO, LHI, C1, C2):
            halo(kind, now).wait_recv()
        first, last = row_ids() == 0, row_ids() == 7
        up_xy, up_yz, acc_vy = (
            jnp.where(first, lr_hi[now, k], yr_hi[now, k]) for k in range(3)
        )
        dn_yy, acc_vx, acc_vz = (
            jnp.where(first, lr_lo[now, k], yr_lo[now, k]) for k in range(3)
        )
        dex, dey = hy_lo[0, 0:1] * co[0], hx_lo[0, 0:1] * co[0]
        bulk = kc[0] * (dex + dey)
        corner1 = cr[now, 1] + (bulk + (kc[1] + kc[1]) * dex)
        corner2 = cr[now, 2] + (bulk + (kc[1] + kc[1]) * dey)
        corner3 = cr[now, 3] - kc[2] * (hx_lo[0, 15:16] * co[1])
        vx_ym = hy_lo[1] + hy_lo[0] * (acc_vx + g[now, 0] - jnp.where(first, corner1, 0.0))
        vz_ym = hy_lo[2] + hy_lo[0] * (acc_vz + g[now, 1])
        vy_yp = hy_hi[1] + hy_hi[0] * (acc_vy - g[now, 8])
        hy_lo[1], hy_lo[2], hy_hi[1] = vx_ym, vz_ym, vy_yp
        dvy_xm = -hx_lo[0, 0:1] * corner2
        dvz_xm = hx_lo[0, 15:16] * corner3
        hx_lo[1, 0:1] = hx_lo[1, 0:1] + dvy_xm
        hx_lo[2, 15:16] = hx_lo[2, 15:16] + dvz_xm
        dvx, dvz, dvy = fm[2, 1] * up_xy, fm[2, 1] * up_yz, -fm[2, 0] * dn_yy
        gv[0], gv[1], gv[2] = gv[0] + dvx, gv[1] + dvz, gv[2] + dvy
        lam, mu = fm[0, 1], fm[1, 1]
        ex = up_i(dvx) - dvx
        ez = up_z(dvz) - dvz
        bulk = lam * (ex + vy_yp + ez)
        mu2 = mu + mu
        dvz_m = jnp.where(first, dvz_xm, pltpu.roll(dvz, 1, 0))
        xy15 = g[later, 4] + mu * dvx
        xz15 = g[later, 5] + mu * ((dvz - dvz_m) + (dvx - dn_z(dvx)))
        g[later, 3] = g[later, 3] + (bulk + mu2 * ex)
        g[later, 8] = g[later, 8] + (bulk + mu2 * vy_yp)
        g[later, 7] = g[later, 7] + (bulk + mu2 * ez)
        g[later, 4] = xy15
        g[later, 5] = xz15
        g[later, 6] = g[later, 6] + mu * dvz
        lam, mu = fm[0, 0], fm[1, 0]
        bulk = lam * dvy
        dvy_m = jnp.where(first, dvy_xm, pltpu.roll(dvy, 1, 0))
        xy00 = g[later, 0] + mu * ((dvy - dvy_m) - vx_ym)
        g[later, 9] = g[later, 9] - bulk
        g[later, 10] = g[later, 10] - bulk
        g[later, 2] = g[later, 2] - (bulk + (mu + mu) * dvy)
        g[later, 0] = xy00
        g[later, 1] = g[later, 1] + mu * ((dvy - dn_z(dvy)) - vz_ym)

        @pl.when(t < STEPS - 1)
        def _():
            for kind in (C1, C2):
                halo(kind, now).wait_send()
            send_corners(later)

        for kind in (C0, C3):
            halo(kind, now).wait_recv()
        corner0, corner4 = cr[now, 0], cr[now, 4]
        dvx_xp = hx_hi[0, 15:16] * corner0
        hx_hi[1, 15:16] = hx_hi[1, 15:16] + dvx_xp
        dvy_yp = hy_hi[0, 7:8] * corner0
        hy_hi[1, 7:8] = hy_hi[1, 7:8] + dvy_yp
        dvz_ym = hy_lo[0, 7:8] * corner4
        hy_lo[2, 7:8] = hy_lo[2, 7:8] + dvz_ym
        lam, mu2 = fm[0, 1, 7:8], fm[1, 1, 7:8] + fm[1, 1, 7:8]
        bulk = lam * (dvx_xp + dvy_yp)
        g[later, 3, 7:8] = g[later, 3, 7:8] + (bulk + mu2 * dvx_xp)
        g[later, 8, 7:8] = g[later, 8, 7:8] + (bulk + mu2 * dvy_yp)
        g[later, 7, 7:8] = g[later, 7, 7:8] + bulk
        g[later, 1, 7:8] = g[later, 1, 7:8] - fm[1, 0, 7:8] * dvz_ym

        @pl.when(t < STEPS - 1)
        def _():
            for kind in (YLO, YHI):
                halo(kind, now).wait_send()
            send_lines(later)
            for kind in LATE:
                halo(kind, now).wait_send()
            sums_wait(now, send_sem.at[SUMS])
            co[0], co[1] = cs[0], cs[4]

        def patch(row, line0, line15):
            low = row[:8] if line0 is None else jnp.where(first, line0, row[:8])
            return jnp.concatenate([low, jnp.where(last, line15, row[8:])], axis=0)

        xy0 = patch(xy_row, xy00[0:1], xy15[0:1])
        xz0 = patch(xz_row, None, xz15[0:1])
        trial_y = nodes(xy0) + face[0]
        trial_z = nodes(xz0) + face[1]
        mag = jnp.sqrt(trial_y * trial_y + trial_z * trial_z)
        load_ratio = face[2] / mag
        rate = mag * face[3]

        @pl.when(t == STEPS - 1)
        def _():
            write_back(later)
            out_copy(0).start()
            out_copy(1).start()

        sums_wait(now, recv_sem.at[SUMS, now])
        total = jnp.zeros(wide, jnp.float32)
        for q in range(4):
            part = ar[now, 4 * q] + ar[now, 4 * q + 1] + ar[now, 4 * q + 2] + ar[now, 4 * q + 3]
            total = total + same[:, q * LANES : (q + 1) * LANES] * part
        seg_sum = jnp.sum(total, axis=1, keepdims=True)
        friction = coef[2] + coef[1] * jnp.exp(seg_sum * coef[0])
        excess = 1.0 - jnp.minimum(friction * load_ratio, 1.0)
        slip_now = sn[...] + rate * excess
        sn[...] = slip_now
        dy, dz = face_of(trial_y * excess), face_of(trial_z * excess)
        xy, xz = xy0 - dy, xz0 - dz
        s[3, 0] = xy
        s[4, 0] = xz
        g[later, 0, 0:1], g[later, 4, 0:1], g[later, 5, 0:1] = xy[0:1], xy[15:], xz[15:]

        @pl.when(t < STEPS - 1)
        def _():
            send_late(later, xy, xz, dy, dz, slip_now)

        @pl.when(t < STEPS - 1)
        def _():
            write_back(later)
            send_rows(later)

        return carry

    lax.fori_loop(0, STEPS, advance, 0)

    slip[...] = face_of(sn[...])
    out_copy(2).start()
    out_copy(3).start()
    for kind in EARLY + LATE:
        halo(kind, 0).wait_send()
    sums_wait(0, send_sem.at[SUMS])
    for copy in once_copies():
        copy.wait_send()
    for k in range(len(outs)):
        out_copy(k).wait()


def hand_over(vel_i, str_i, slip_i, vel_o, str_o, slip_o, v, s, slip, in_sem, out_sem):
    pieces = [(vel_i.at[k], v.at[k], vel_o.at[k]) for k in range(3)]
    pieces += [(str_i.at[k], s.at[k], str_o.at[k]) for k in range(6)]
    pieces.append((slip_i, slip, slip_o))
    ins = [pltpu.make_async_copy(a, b, in_sem.at[k]) for k, (a, b, _) in enumerate(pieces)]
    outs = [pltpu.make_async_copy(b, c, out_sem.at[k]) for k, (_, b, c) in enumerate(pieces)]
    for copy in ins:
        copy.start()
    for copy, out in zip(ins, outs):
        copy.wait()
        out.start()
    for out in outs:
        out.wait()


def on_device(*args):
    f32 = jnp.float32
    vm = pltpu.VMEM
    block = (CX, NY, NZ)
    scratch = [
        vm((3, *block), f32), vm((6, *block), f32), vm((3, *block), f32),
        vm((2, NY, NZ), f32), vm((NY, NZ), f32), vm((NY, NZ), f32),
        vm((1, SEGS), f32), vm((1, SEGS), f32), vm((1, SEGS), f32),
        vm((SEGS, MAXB), jnp.int32),
        vm((BLOCKS, TOTAL), f32), vm((3, BLOCKS, LANES), f32), vm((4, BLOCKS, LANES), f32),
        vm((BLOCKS, LANES), f32), vm((SLOTS, len(LINES), CX, NZ), f32),
        vm((3, CX, NZ), f32), vm((3, 2, CX, NZ), f32),
        vm((3, NY, NZ), f32), vm((3, NY, NZ), f32), vm((3, CX, NZ), f32), vm((3, CX, NZ), f32),
        vm((3, 1, NZ), f32), vm((3, 1, NZ), f32), vm((5, 1, NZ), f32),
        vm((2, 1, NZ), f32),
        vm((2, NY, NZ), f32), vm((3, NY, NZ), f32), vm((2, CX, NZ), f32), vm((3, CX, NZ), f32),
        vm((3, 1, NZ), f32),
        vm((SLOTS, 3, NY, NZ), f32), vm((SLOTS, 3, NY, NZ), f32),
        vm((SLOTS, 3, CX, NZ), f32), vm((SLOTS, 3, CX, NZ), f32),
        vm((SLOTS, 3, 1, NZ), f32), vm((SLOTS, 3, 1, NZ), f32),
        vm((SLOTS, 5, 1, NZ), f32), vm((SLOTS, GY, 1, LANES), f32),
        vm((3, NY, NZ), f32), vm((2, NY, NZ), f32), vm((3, CX, NZ), f32), vm((2, CX, NZ), f32),
        vm((3, 1, NZ), f32),
        pltpu.SemaphoreType.DMA((10,)), pltpu.SemaphoreType.DMA((11,)),
        pltpu.SemaphoreType.DMA((11, SLOTS)), pltpu.SemaphoreType.DMA((6,)),
        pltpu.SemaphoreType.DMA((6,)), pltpu.SemaphoreType.DMA((4,)),
    ]
    anywhere = pl.BlockSpec(memory_space=pltpu.HBM)
    shapes = (
        jax.ShapeDtypeStruct((3, *block), f32),
        jax.ShapeDtypeStruct((6, *block), f32),
        jax.ShapeDtypeStruct((1, NY, NZ), f32),
    )
    results = pl.pallas_call(
        kernel,
        out_shape=shapes,
        in_specs=[anywhere] * 10,
        out_specs=(anywhere,) * 3,
        scratch_shapes=scratch,
        compiler_params=pltpu.CompilerParams(
            collective_id=0, has_side_effects=True, vmem_limit_bytes=62 << 20
        ),
        name="fault_steps",
    )(*args)
    return pl.pallas_call(
        hand_over,
        out_shape=shapes,
        in_specs=[anywhere] * 3,
        out_specs=(anywhere,) * 3,
        scratch_shapes=[
            vm((3, *block), f32), vm((6, *block), f32), vm((1, NY, NZ), f32),
            pltpu.SemaphoreType.DMA((10,)), pltpu.SemaphoreType.DMA((10,)),
        ],
        compiler_params=pltpu.CompilerParams(vmem_limit_bytes=62 << 20),
        name="hand_over",
    )(*results)


def solution(mesh):
    wave = P(None, "gx", "gy", None)
    fault = P("gx", "gy", None)
    row = P("gx", None)
    return jax.shard_map(
        on_device,
        mesh=mesh,
        in_specs=(wave, wave, wave, wave, fault, fault, row, row, row, P("gx", None, None)),
        out_specs=(wave, wave, fault),
        check_vma=False,
    )
```
